32 devices in a mesh: depth: 2 (over x), wide: 16 (over z, y, core).
Axes of the slice: x: 2, y: 2, z: 4, core: 2. Of those that a mesh axis runs over, the one named last changes fastest.
Arguments:
- volume: bfloat16 [256, 128, 1024], P(('depth', 'wide')), may hold values from -6 to 6
- directions: int32 [2, 128], replicated, may hold values from 0 to 1
- light_dir: float32 [2, 3], replicated, may hold values from -4 to 4
- tf_center: float32 [2, 4], replicated, may hold values from -1.5 to 1.5
- tf_width: float32 [2, 4], replicated, may hold values from 0.2 to 0.8
- tf_height: float32 [2, 4], replicated, may hold values from 0.25 to 4
- tf_emission: float32 [2, 4, 3], replicated, may hold values from 0.5 to 6
Outputs:
- image_rgba: float32 [2, 4, 131072], P(None, None, ('depth', 'wide'))
The draws below stay inside these ranges and needn't reach their ends.
Inputs may be any that keep to these rules, and one draw needn't show every extreme that they name: `directions`: 0 marks rays that run toward increasing depth index, 1 rays that run toward decreasing depth index.
All inputs are finite; a program needn't handle non-finite values.
Results may differ from the reference program's by a relative error of at most 0.0003.
Values may be sent and summed in bfloat16 or wider, within the bound.
A program may use at most 64 MiB of HBM per device.

```python
import math
import jax
import jax.numpy as jnp
from jax import lax

IW = 1024
IH = 128
VIEWS = 2
BUMPS = 4
NZ = 256


def place_ends(drawn, key, low, high):
    spot = [jax.random.randint(jax.random.fold_in(key, axis), (), 0, length) for axis, length in enumerate(drawn.shape)]
    main_axis = drawn.shape.index(max(drawn.shape))
    beside = spot[:main_axis] + [(spot[main_axis] + 1) % drawn.shape[main_axis]] + spot[main_axis + 1:]
    return drawn.at[tuple(spot)].set(low).at[tuple(beside)].set(high)


def steps_of(rng, shape, cuts, low, largest):
    def one(position, parts):
        heights = jax.random.uniform(jax.random.fold_in(jax.random.fold_in(rng, 6), position), (parts,), jnp.float32, low / len(cuts), largest / len(cuts))
        return jnp.repeat(jnp.exp(heights), shape[position] // parts).reshape((-1,) + (1,) * (len(shape) - position - 1))

    level = one(*cuts[0])
    for cut in cuts[1:]:
        level = level * one(*cut)
    return level


def centred(key, dims, deviation, reach, cuts=(), held_as=jnp.bfloat16):
    array = deviation * jax.random.normal(key, dims, jnp.float32)
    if cuts:
        array = array * steps_of(key, dims, cuts, -0.22, 0.18)
    return jnp.clip(array, -reach, reach).astype(held_as)


def setup_inputs(seed: int = 0) -> dict:
    streams_of = jax.random.split(jax.random.key(seed), 8)
    return {
        "volume": centred(streams_of[0], (NZ, IH, IW), 1.0, 6.0, ((0, 32),)),
        "directions": place_ends(jax.random.randint(streams_of[1], (VIEWS, IH), 0, 2), jax.random.fold_in(streams_of[1], 1), 0, 1).astype(jnp.int32),
        "light_dir": centred(streams_of[2], (VIEWS, 3), 1.0, 4.0, (), jnp.float32),
        "tf_center": jnp.clip(jax.random.uniform(streams_of[3], (VIEWS, BUMPS), jnp.float32, -1.5, 1.5), -1.5, 1.5),
        "tf_width": jnp.clip(jax.random.uniform(streams_of[4], (VIEWS, BUMPS), jnp.float32, 0.2, 0.8), 0.2, 0.8),
        "tf_height": jnp.clip(jnp.exp(jax.random.uniform(streams_of[5], (VIEWS, BUMPS), jnp.float32, math.log(0.25), math.log(4.0))), 0.25, 4.0),
        "tf_emission": jnp.clip(jax.random.uniform(streams_of[6], (VIEWS, BUMPS, 3), jnp.float32, 0.5, 6.0), 0.5, 6.0),
    }


AMBIENT = 0.3
DIFFUSE = 0.7

def shifted_diff(values, along_axis):
    padding = [(0, 0)] * values.ndim
    padding[along_axis] = (1, 1)
    padded = jnp.pad(values, padding)
    length_now = values.shape[along_axis]
    upper_part = lax.slice_in_dim(padded, 2, length_now + 2, 1, along_axis)
    lower_part = lax.slice_in_dim(padded, 0, length_now, 1, along_axis)
    return 0.5 * (upper_part - lower_part)

def layer_rgba(layer_below, center_layer, layer_above, light_dir, tf_center, tf_width, tf_height, tf_emission, depth_step):
    grad_z = 0.5 * (layer_above - layer_below)
    grad_y = shifted_diff(center_layer, 0)
    grad_x = shifted_diff(center_layer, 1)
    lighting = jnp.abs(grad_z[None] * light_dir[:, 0, None, None] + grad_y[None] * light_dir[:, 1, None, None] + grad_x[None] * light_dir[:, 2, None, None])
    magnitude = jnp.sqrt(grad_x * grad_x + grad_y * grad_y + grad_z * grad_z + 1.0)
    shading = AMBIENT + DIFFUSE * lighting / magnitude[None]
    scaled = (center_layer[None, None] - tf_center[:, :, None, None]) / tf_width[:, :, None, None]
    bumps = jnp.exp(-scaled * scaled)
    density = lax.optimization_barrier(jnp.sum(tf_height[:, :, None, None] * bumps, axis=1))
    weights = tf_height[:, :, None] * tf_emission
    tinted = jnp.einsum('vkc,vkhw->vchw', weights, bumps, precision=lax.Precision.HIGHEST)
    colour = depth_step * shading[:, None] * tinted
    opacity = 1.0 - jnp.exp(-depth_step * density)
    sample_rgba = jnp.concatenate([colour, opacity[:, None]], axis=1)
    return sample_rgba.reshape(sample_rgba.shape[0], 4, -1)

def over_ordered(lower_part, upper_part, flags):
    front_first = lower_part + (1.0 - lower_part[:, 3:4]) * upper_part
    back_first = upper_part + (1.0 - upper_part[:, 3:4]) * lower_part
    return jnp.where(flags, back_first, front_first)

def reference(volume, directions, light_dir, tf_center, tf_width, tf_height, tf_emission):
    layer_total = volume.shape[0]
    depth_step = 1.0 / layer_total
    padded = jnp.pad(volume, ((1, 1), (0, 0), (0, 0)))
    flags = jnp.repeat(directions == 1, volume.shape[2], axis=1)[:, None, :]

    def advance(composite, layer_index):
        layers = lax.dynamic_slice_in_dim(padded, layer_index, 3, 0).astype(jnp.float32)
        sample_rgba = layer_rgba(layers[0], layers[1], layers[2], light_dir, tf_center, tf_width, tf_height, tf_emission, depth_step)
        return (over_ordered(composite, sample_rgba, flags), None)
    initial = jnp.zeros((light_dir.shape[0], 4, volume.shape[1] * volume.shape[2]), jnp.float32)
    composite, unused = lax.scan(advance, initial, jnp.arange(layer_total, dtype=jnp.int32))
    return composite
```

```python
import functools
import math

import jax
import jax.numpy as jnp
from jax import lax
from jax.experimental import pallas as pl
from jax.experimental.pallas import tpu as pltpu
from jax.sharding import PartitionSpec as P

AMBIENT = 0.3
DIFFUSE = 0.7


def padded_2(block, sides, width):
    for axis, dim in sides:
        count = lax.axis_size(axis)
        forward = [(i, i + 1) for i in range(count - 1)]
        backward = [(target, source) for source, target in forward]
        low = lax.ppermute(
            lax.slice_in_dim(block, block.shape[dim] - width, None, axis=dim), axis, forward
        )
        high = lax.ppermute(lax.slice_in_dim(block, 0, width, axis=dim), axis, backward)
        block = jnp.concatenate([low, block, high], axis=dim)
    return block


def partner(block, axis, distance):
    count = lax.axis_size(axis)
    route = []
    for low in range(count):
        high = low | 1 << distance
        if high != low and high < count:
            route += [(low, high), (high, low)]
    return lax.ppermute(block, axis, route)


def shifted_diff(values, along_axis):
    padding = [(0, 0)] * values.ndim
    padding[along_axis] = (1, 1)
    padded = jnp.pad(values, padding)
    length_now = values.shape[along_axis]
    upper_part = lax.slice_in_dim(padded, 2, length_now + 2, 1, along_axis)
    lower_part = lax.slice_in_dim(padded, 0, length_now, 1, along_axis)
    return 0.5 * (upper_part - lower_part)


def layer_rgba(
    layer_below,
    center_layer,
    layer_above,
    light_dir,
    tf_center,
    tf_width,
    tf_height,
    tf_emission,
    depth_step,
):
    grad_z = 0.5 * (layer_above - layer_below)
    grad_y = shifted_diff(center_layer, 0)
    grad_x = shifted_diff(center_layer, 1)
    lighting = jnp.abs(
        grad_z[None] * light_dir[:, 0, None, None]
        + grad_y[None] * light_dir[:, 1, None, None]
        + grad_x[None] * light_dir[:, 2, None, None]
    )
    magnitude = jnp.sqrt(grad_x * grad_x + grad_y * grad_y + grad_z * grad_z + 1.0)
    shading = AMBIENT + DIFFUSE * lighting / magnitude[None]
    scaled = (center_layer[None, None] - tf_center[:, :, None, None]) / tf_width[:, :, None, None]
    bumps = jnp.exp(-scaled * scaled)
    density = jnp.sum(tf_height[:, :, None, None] * bumps, axis=1)
    weights = tf_height[:, :, None] * tf_emission
    tinted = jnp.einsum("vkc,vkhw->vchw", weights, bumps, precision=lax.Precision.HIGHEST)
    colour = depth_step * shading[:, None] * tinted
    opacity = 1.0 - jnp.exp(-depth_step * density)
    sample_rgba = jnp.concatenate([colour, opacity[:, None]], axis=1)
    return sample_rgba.reshape(sample_rgba.shape[0], 4, -1)


def over_ordered(lower_part, upper_part, flags):
    front_first = lower_part + (1.0 - lower_part[:, 3:4]) * upper_part
    back_first = upper_part + (1.0 - upper_part[:, 3:4]) * lower_part
    return jnp.where(flags, back_first, front_first)


def split_pair(values, along_axis):
    array_shape = values.shape
    new_shape = (
        array_shape[:along_axis] + (array_shape[along_axis] // 2, 2) + array_shape[along_axis + 1 :]
    )
    paired = values.reshape(new_shape)
    first_half = lax.index_in_dim(paired, 0, along_axis + 1, keepdims=False)
    second_half = lax.index_in_dim(paired, 1, along_axis + 1, keepdims=False)
    return (first_half, second_half)


def plain_body(volume, directions, light_dir, tf_center, tf_width, tf_height, tf_emission):
    depth_count = lax.axis_size("depth")
    wide_count = lax.axis_size("wide")
    slab_cells = volume.shape[0]
    depth_step = 1.0 / (slab_cells * depth_count * wide_count)
    view_count = light_dir.shape[0]
    pixel_count = volume.shape[1] * volume.shape[2]
    flags = jnp.repeat(directions == 1, volume.shape[2], axis=1)[:, None, :]
    padded = padded_2(volume, ((("depth", "wide"), 0),), 1)

    def advance(layer_index, composite):
        layers = lax.dynamic_slice_in_dim(padded, layer_index, 3, 0).astype(jnp.float32)
        sample_rgba = layer_rgba(
            layers[0],
            layers[1],
            layers[2],
            light_dir,
            tf_center,
            tf_width,
            tf_height,
            tf_emission,
            depth_step,
        )
        return over_ordered(composite, sample_rgba, flags)

    initial = jnp.zeros((view_count, 4, pixel_count), jnp.float32)
    slab_image = lax.fori_loop(0, slab_cells, advance, initial)
    block_pixels = pixel_count // (depth_count * wide_count)
    blocked = slab_image.reshape(view_count, 4, depth_count, wide_count, block_pixels)
    blocked_flags = flags.reshape(view_count, 1, depth_count, wide_count, block_pixels)
    wide_index = lax.axis_index("wide")
    depth_index = lax.axis_index("depth")
    merged = blocked
    merged_flags = blocked_flags
    for bit_number in range(wide_count.bit_length() - 1):
        own_bit = wide_index >> bit_number & 1
        first_half, second_half = split_pair(merged, 3)
        flag_first, flag_second = split_pair(merged_flags, 3)
        kept = jnp.where(own_bit == 0, first_half, second_half)
        outgoing = jnp.where(own_bit == 0, second_half, first_half)
        merged_flags = jnp.where(own_bit == 0, flag_first, flag_second)
        incoming = partner(outgoing, "wide", bit_number)
        merged = jnp.where(
            own_bit == 0,
            over_ordered(kept, incoming, merged_flags),
            over_ordered(incoming, kept, merged_flags),
        )
    range_image = jnp.squeeze(merged, 3)
    range_flags = jnp.squeeze(merged_flags, 3)
    merged = range_image
    merged_flags = range_flags
    for bit_number in range(depth_count.bit_length() - 1):
        own_bit = depth_index >> bit_number & 1
        first_half, second_half = split_pair(merged, 2)
        flag_first, flag_second = split_pair(merged_flags, 2)
        kept = jnp.where(own_bit == 0, first_half, second_half)
        outgoing = jnp.where(own_bit == 0, second_half, first_half)
        merged_flags = jnp.where(own_bit == 0, flag_first, flag_second)
        incoming = partner(outgoing, "depth", bit_number)
        merged = jnp.where(
            own_bit == 0,
            over_ordered(kept, incoming, merged_flags),
            over_ordered(incoming, kept, merged_flags),
        )
    final_block = jnp.squeeze(merged, 2)
    return final_block


MESH = pl.DeviceIdType.MESH
LOG2E = math.log2(math.e)
LANES = 256
TILES = LANES // 128
QUARTERS = 4
CHUNKS = 32
EARLY = 8
GREET = 3
LAG_CORE, LAG_QUAD, LAG_LAST = 2, 3, 16
LAST_IN_LOOP = 1
CODE_SCALE = 2048.0
CODE_SHIFT = 26.0


def encode(first, second):
    def code(value):
        at = jnp.log2(value) * CODE_SCALE + (CODE_SHIFT * CODE_SCALE + 0.5)
        return jnp.clip(at, 0.0, 65535.0).astype(jnp.int32)

    return code(first) | (code(second) << 16)


def decode(word):
    low = (word & 65535).astype(jnp.float32)
    high = ((word >> 16) & 65535).astype(jnp.float32)
    return [part * (1.0 / CODE_SCALE) - CODE_SHIFT for part in (low, high)]


def composite(words, flag):
    logs = [decode(a) + decode(b) for a, b in words]
    thick = [jnp.exp2(part[3]) for part in logs]
    before = [jnp.zeros_like(thick[0])]
    for t in thick:
        before.append(before[-1] + t)
    total = before[-1]
    colours = None
    for s, part in enumerate(logs):
        hidden = jnp.where(flag, total - before[s + 1], before[s])
        terms = [jnp.exp2(part[ch] - hidden) for ch in range(3)]
        colours = terms if colours is None else [a + b for a, b in zip(colours, terms)]
    return colours, total


def kernel(
    layer_total,
    vol, dirs_in, light_in, center_in, width_in, height_in, tint_in,
    out,
    slabs, dirs, light, center, width, height, tint, in_sems,
    xf, halo, flagv, flago, cst, early, rbuf, cbuf, abuf, bbuf,
    halo_ss, halo_rs, core_ss, core_rs, quad_ss, quad_rs, last_ss, last_rs,
):
    slab, rows, cols = vol.shape
    step = 1.0 / layer_total
    x = lax.axis_index("depth")
    w = lax.axis_index("wide")
    c = lax.rem(w, 2)
    y = lax.rem(lax.div(w, 2), 2)
    z0 = lax.rem(lax.div(w, 4), 2)
    z1 = lax.div(w, 8)
    me = x * 16 + w
    quad = z0 * 2 + y
    half = x * 2 + z1
    core_peer = (x, w + 1 - 2 * c)

    def quad_dev(rel):
        ry = lax.rem(rel, 2)
        rz = lax.div(rel, 2)
        return (x, w + ry * (2 - 4 * y) + rz * (4 - 8 * z0))

    def last_dev(b5, b2):
        return (c, b5 * 8 + z0 * 4 + y * 2 + b2)

    def last_mine(b5, b2):
        return jnp.logical_and(x == c, jnp.logical_and(b5 == z1, b2 == c))

    outer = lax.rem(me + 31 + 2 * c, 32)
    outer_dev = (lax.div(outer, 16), lax.rem(outer, 16))
    has_outer = jnp.logical_or(jnp.logical_and(c == 0, me > 0), jnp.logical_and(c == 1, me < 31))

    given = (
        (dirs_in, dirs), (light_in, light), (center_in, center), (width_in, width),
        (height_in, height), (tint_in, tint),
    )
    small = [pltpu.make_async_copy(a, b, in_sems.at[n]) for n, (a, b) in enumerate(given)]

    def slab_copy(z):
        return pltpu.make_async_copy(vol.at[z], slabs.at[z], in_sems.at[6 + z])

    barrier = pltpu.get_barrier_semaphore()

    def greet(device):
        pl.semaphore_signal(barrier, inc=1, device_id=device, device_id_type=MESH)

    @pl.when(has_outer)
    def _():
        greet(outer_dev)

    for sx in range(2):
        for sz in range(2):
            @pl.when(jnp.logical_not(jnp.logical_and(x == c, jnp.logical_and(sx == x, sz == z1))))
            def _():
                greet((sx, sz * 8 + z0 * 4 + y * 2 + x))
    for rel in (3, 2, 1):
        greet(quad_dev(rel))
    greet(core_peer)
    for z in range(slab):
        slab_copy(z).start()
    for copy in small:
        copy.start()

    def halo_lanes(q):
        return pl.ds(pl.multiple_of(q * LANES, LANES), LANES)

    def outer_copy(q):
        return pltpu.make_async_remote_copy(
            src_ref=vol.at[c * (slab - 1), :, halo_lanes(q)], dst_ref=halo.at[1 - c, q],
            send_sem=halo_ss.at[0], recv_sem=halo_rs.at[0, q],
            device_id=outer_dev, device_id_type=MESH)

    def inner_copy(q):
        return pltpu.make_async_remote_copy(
            src_ref=vol.at[(1 - c) * (slab - 1), :, halo_lanes(q)], dst_ref=halo.at[c, q],
            send_sem=halo_ss.at[1], recv_sem=halo_rs.at[1, q],
            device_id=core_peer, device_id_type=MESH)

    blank_rows = jnp.zeros((8, 128), jnp.float32)

    def blank(z, carry):
        for b in range(rows // 8 + 2):
            xf[z, 0, b * 8:b * 8 + 8, :] = blank_rows
            xf[z, cols // 128 + 1, b * 8:b * 8 + 8, :] = blank_rows
        for t in range(cols // 128):
            xf[z, t + 1, 0:8, :] = blank_rows
            xf[z, t + 1, rows + 8:rows + 16, :] = blank_rows
        return carry

    lax.fori_loop(1, slab + 1, blank, 0)

    def pad(z, carry):
        slab_copy(z - 1).wait()

        def widen(b, inner):
            for t in range(cols // 128):
                for r in (0, 16):
                    xf[z, t + 1, pl.ds(pl.multiple_of(b * 32 + r + 8, 8), 16), :] = slabs[
                        z - 1, pl.ds(pl.multiple_of(b * 32 + r, 16), 16), t * 128:t * 128 + 128
                    ].astype(jnp.float32)
            return inner

        return lax.fori_loop(0, rows // 32, widen, carry)

    lax.fori_loop(1, slab + 1, pad, 0)

    for copy in small:
        copy.wait()
    for v in range(2):
        for k in range(4):
            full = lambda ref: jnp.full((8, 128), ref[v, k], jnp.float32)
            scale = math.sqrt(LOG2E) / full(width)
            cst[v * 15 + k] = scale
            cst[v * 15 + 4 + k] = scale * full(center)
            cst[v * 15 + 8 + k] = jnp.log(full(height) * (step * LOG2E)) * LOG2E
        for a in range(3):
            cst[v * 15 + 12 + a] = jnp.full((8, 128), DIFFUSE * light[v, a], jnp.float32)
    row_of = lax.broadcasted_iota(jnp.int32, (8, 128), 0)
    lane_of = lax.broadcasted_iota(jnp.int32, (8, 128), 1)

    def fill_flags(g, carry):
        for v in range(2):
            for i in range(8):
                flagv[v, g, i:i + 1, :] = jnp.full((1, 128), dirs[v, g * 8 + i].astype(jnp.float32))
        return carry

    lax.fori_loop(0, rows // 8, fill_flags, 0)
    value = jnp.zeros((8, 128), jnp.float32)
    for i in range(8):
        value = jnp.where(row_of == i, dirs[i // 4, me * 4 + i % 4].astype(jnp.float32), value)
    flago[...] = value

    def take_halo(side, present, copy, q):
        place = side * (slab + 1)

        @pl.when(present)
        def _():
            copy(q).wait_recv()
            for p in range(TILES):
                xf[place, q * TILES + p + 1, 8:rows + 8, :] = halo[
                    side, q, :, p * 128:p * 128 + 128].astype(jnp.float32)

        @pl.when(jnp.logical_not(present))
        def _():
            for p in range(TILES):
                xf[place, q * TILES + p + 1, 8:rows + 8, :] = jnp.zeros((rows, 128), jnp.float32)

    def where_is(k):
        m = jnp.where(k < 6, k, jnp.where(k < 30, lax.rem(k + 2, 8), k - 24))
        b = jnp.where(k < 6, 0, jnp.where(k < 30, lax.div(k + 2, 8), 4))
        own = m >= 6
        q = jnp.where(own, b - 1, b)
        b5 = jnp.where(own, m - 6, jnp.where(m >= 3, 1, 0))
        rel = jnp.where(own, 0, 3 - m + 3 * b5)
        odd = jnp.logical_or(rel == 1, rel == 3)
        to_y = jnp.where(odd, 1 - y, y)
        to_z = jnp.where(rel >= 2, 1 - z0, z0)
        return q, b5, rel, b5 * 4 + to_z * 2 + to_y

    def layer(z, t, r0, here, behind, ahead, flags, signs, run, sums):
        rows8 = pl.ds(r0, 8)
        left = xf[z, t, rows8, :]
        right = xf[z, t + 2, rows8, :]
        above = xf[z, t + 1, pl.ds(r0 - 1, 8), :]
        below = xf[z, t + 1, pl.ds(r0 + 1, 8), :]
        gz = ahead - behind
        gy = below - above
        gx = pltpu.roll(jnp.where(lane_of == 0, right, here), 127, 1) - pltpu.roll(
            jnp.where(lane_of == 127, left, here), 1, 1)
        inverse = lax.rsqrt(gx * gx + gy * gy + (gz * gz + 4.0))
        for v in range(2):
            dot = gz * cst[v * 15 + 12] + gy * cst[v * 15 + 13] + gx * cst[v * 15 + 14]
            shade = jnp.abs(dot) * inverse + AMBIENT
            bumps = []
            for b in range(4):
                u = here * cst[v * 15 + b] - cst[v * 15 + 4 + b]
                bumps.append(jnp.exp2(cst[v * 15 + 8 + b] - u * u))
            thick = (bumps[0] + bumps[1]) + (bumps[2] + bumps[3])
            if run[v] is None:
                later = signs[v] * thick
                weight = jnp.exp2(jnp.where(flags[v], later, 0.0)) * shade
            else:
                later = run[v] + signs[v] * thick
                weight = jnp.exp2(jnp.where(flags[v], later, run[v])) * shade
            run[v] = later
            if sums[v] is None:
                sums[v] = [weight * b for b in bumps]
            else:
                sums[v] = [s + weight * b for s, b in zip(sums[v], bumps)]

    def tile_place(q, g, t):
        h = jnp.where(t >= TILES, 1, 0)
        p = t - TILES * h
        row_tile = h * 8 + g
        return h, p, row_tile, q * TILES + p, pl.multiple_of(row_tile * 8 + 8, 8)

    def orient(row_tile):
        flags = [flagv[v, row_tile] > 0.5 for v in range(2)]
        return flags, [jnp.where(f, 1.0, -1.0) for f in flags]

    def inside(first, last, t, r0, flags, signs, run, sums):
        rows8 = pl.ds(r0, 8)
        behind = xf[first - 1, t + 1, rows8, :]
        here = xf[first, t + 1, rows8, :]
        for z in range(first, last + 1):
            ahead = xf[z + 1, t + 1, rows8, :]
            layer(z, t, r0, here, behind, ahead, flags, signs, run, sums)
            behind, here = here, ahead

    def begin(k):
        q, b5, rel, g = where_is(k)

        def tile(t, carry):
            h, p, row_tile, lane_tile, r0 = tile_place(q, g, t)
            flags, signs = orient(row_tile)
            run, sums = [None, None], [None, None]
            inside(2, slab - 1, lane_tile, r0, flags, signs, run, sums)
            for v in range(2):
                for b in range(4):
                    early[k, t, v * 5 + b] = sums[v][b]
                early[k, t, v * 5 + 4] = run[v]
            return carry

        lax.fori_loop(0, 2 * TILES, tile, 0)

    def finish(k, whole):
        q, b5, rel, g = where_is(k)

        def tile(t):
            h, p, row_tile, lane_tile, r0 = tile_place(q, g, t)
            flags, signs = orient(row_tile)
            run, sums = [None, None], [None, None]
            if whole:
                inside(1, slab, lane_tile, r0, flags, signs, run, sums)
            else:
                inside(1, 1, lane_tile, r0, flags, signs, run, sums)
                for v in range(2):
                    lift = jnp.exp2(run[v])
                    sums[v] = [s + lift * early[k, t, v * 5 + b] for b, s in enumerate(sums[v])]
                    run[v] = run[v] + early[k, t, v * 5 + 4]
                inside(slab, slab, lane_tile, r0, flags, signs, run, sums)
            for v in range(2):
                total = signs[v] * run[v]
                front = jnp.where(flags[v], jnp.exp2(-total), 1.0) * (1.0 / LOG2E)
                scaled = [s * front for s in sums[v]]
                for ch in range(3):
                    value = scaled[0] * tint[ch, v, 0]
                    for b in range(1, 4):
                        value = value + scaled[b] * tint[ch, v, b]
                    rbuf[h, k, v, ch, p] = value
                rbuf[h, k, v, 3, p] = total

        def tiles(n, carry):
            for m in range(side):
                tile(n * side + m)
            return carry

        side = 1 if whole else 2
        lax.fori_loop(0, 2 * TILES // side, tiles, 0)

    def core_copy(k):
        return pltpu.make_async_remote_copy(
            src_ref=rbuf.at[1 - c, k], dst_ref=cbuf.at[k], send_sem=core_ss,
            recv_sem=core_rs.at[k], device_id=core_peer, device_id_type=MESH)

    def quad_copy(rel, n):
        return pltpu.make_async_remote_copy(
            src_ref=abuf.at[3 + rel, n], dst_ref=abuf.at[quad, n], send_sem=quad_ss.at[rel - 1],
            recv_sem=quad_rs.at[rel - 1, n], device_id=quad_dev(rel), device_id_type=MESH)

    def last_copy(b5, b2, q):
        return pltpu.make_async_remote_copy(
            src_ref=bbuf.at[4 + b5 * 2 + b2, q], dst_ref=bbuf.at[half, q],
            send_sem=last_ss.at[b5 * 2 + b2], recv_sem=last_rs.at[half, q],
            device_id=last_dev(b5, b2), device_id_type=MESH)

    side_of_core = c.astype(jnp.float32)

    def merge_core(k):
        q, b5, rel, g = where_is(k)
        n = b5 * QUARTERS + q
        slot = jnp.where(rel == 0, quad, 3 + rel)
        core_copy(k).wait_recv()
        for v in range(2):
            flag = jnp.abs(flagv[v, c * 8 + g] - side_of_core) > 0.5
            for p in range(TILES):
                mine = [rbuf[c, k, v, ch, p] for ch in range(4)]
                other = [cbuf[k, v, ch, p] for ch in range(4)]
                clear = jnp.exp2(-jnp.where(flag, other[3], mine[3]))
                for_mine = jnp.where(flag, clear, 1.0)
                for_other = jnp.where(flag, 1.0, clear)
                colour = [for_mine * mine[ch] + for_other * other[ch] for ch in range(3)]
                abuf[slot, n, v, 0, p] = encode(colour[0], colour[1])
                abuf[slot, n, v, 1, p] = encode(colour[2], mine[3] + other[3])

        @pl.when(rel > 0)
        def _():
            quad_copy(rel, n).start()

    def merge_quad(b5, q):
        n = b5 * QUARTERS + q
        for rel in (3, 2, 1):
            quad_copy(rel, n).wait_recv()
        g = b5 * 4 + quad
        slots = [jnp.where(last_mine(b5, b2), half, 4 + b5 * 2 + b2) for b2 in range(2)]
        for v in range(2):
            flag = flagv[v, c * 8 + g] > 0.5
            for p in range(TILES):
                colour, thick = composite(
                    [(abuf[s, n, v, 0, p], abuf[s, n, v, 1, p]) for s in range(4)], flag)
                first = encode(colour[0], colour[1])
                second = encode(colour[2], thick)
                for b2 in range(2):
                    bbuf[slots[b2], q, 0, p, v * 4:v * 4 + 4] = first[b2 * 4:b2 * 4 + 4]
                    bbuf[slots[b2], q, 1, p, v * 4:v * 4 + 4] = second[b2 * 4:b2 * 4 + 4]
        for b2 in range(2):
            @pl.when(jnp.logical_not(last_mine(b5, b2)))
            def _():
                last_copy(b5, b2, q).start()

    def last_arrived(s, q):
        return pltpu.make_async_remote_copy(
            src_ref=bbuf.at[4, q], dst_ref=bbuf.at[s, q], send_sem=last_ss.at[0],
            recv_sem=last_rs.at[s, q], device_id=core_peer, device_id_type=MESH)

    def merge_last(q):
        for s in range(4):
            @pl.when(jnp.logical_not(jnp.logical_and(x == c, half == s)))
            def _():
                last_arrived(s, q).wait_recv()
        flag = flago[...] > 0.5
        for p in range(TILES):
            colour, thick = composite(
                [(bbuf[s, q, 0, p], bbuf[s, q, 1, p]) for s in range(4)], flag)
            parts = colour + [1.0 - jnp.exp2(-thick)]
            for r in range(8):
                spot = pl.ds(pl.multiple_of((r % 4) * cols + q * LANES + p * 128, 128), 128)
                for ch in range(4):
                    out[r // 4, ch:ch + 1, spot] = parts[ch][r:r + 1, :]

    def open_up():
        pl.semaphore_wait(barrier, 7 + jnp.where(x == c, 0, 1) + jnp.where(has_outer, 1, 0))

    def send_halo(q):
        @pl.when(has_outer)
        def _():
            outer_copy(q).start()

        inner_copy(q).start()

    def before(k, carry):
        @pl.when(k == GREET)
        def _():
            open_up()

        @pl.when(k == GREET)
        def _():
            send_halo(0)

        begin(k)
        return carry

    lax.fori_loop(0, EARLY, before, 0)

    def advance(i, carry):
        @pl.when(i < CHUNKS)
        def _():
            @pl.when(jnp.logical_or(i == 0, jnp.logical_or(i == 6, i == 14)))
            def _():
                send_halo(where_is(i)[0] + 1)

            @pl.when(jnp.logical_or(i == 0, jnp.logical_and(i < 24, lax.rem(i + 2, 8) == 0)))
            def _():
                q = where_is(i)[0]

                @pl.when(c == 0)
                def _():
                    take_halo(0, has_outer, outer_copy, q)
                    take_halo(1, i >= 0, inner_copy, q)

                @pl.when(c == 1)
                def _():
                    take_halo(0, i >= 0, inner_copy, q)
                    take_halo(1, has_outer, outer_copy, q)

            @pl.when(i < EARLY)
            def _():
                finish(i, False)

            @pl.when(i >= EARLY)
            def _():
                finish(i, True)

            core_copy(i).start()

        @pl.when(jnp.logical_and(i >= LAG_CORE, i < CHUNKS + LAG_CORE))
        def _():
            merge_core(i - LAG_CORE)

        @pl.when(jnp.logical_and(i >= LAG_QUAD, i < CHUNKS + LAG_QUAD))
        def _():
            q, b5, rel, g = where_is(i - LAG_QUAD)

            @pl.when(rel == 0)
            def _():
                merge_quad(b5, q)

        @pl.when(jnp.logical_and(i >= LAG_LAST, i < CHUNKS))
        def _():
            q, b5, rel, g = where_is(i - LAG_LAST)

            @pl.when(jnp.logical_and(rel == 0, jnp.logical_and(b5 == 1, q < LAST_IN_LOOP)))
            def _():
                merge_last(q)

        return carry

    lax.fori_loop(0, CHUNKS + LAG_QUAD, advance, 0)

    def close(q, carry):
        merge_last(q)
        return carry

    lax.fori_loop(LAST_IN_LOOP, QUARTERS, close, 0)

    def sent(ref, semaphore):
        pltpu.make_async_remote_copy(
            src_ref=ref, dst_ref=ref, send_sem=semaphore, recv_sem=core_rs.at[0],
            device_id=core_peer, device_id_type=MESH).wait_send()

    sent(rbuf.at[1 - c], core_ss)
    for rel in (1, 2, 3):
        sent(abuf.at[3 + rel], quad_ss.at[rel - 1])
    for b5 in range(2):
        for b2 in range(2):
            @pl.when(jnp.logical_not(last_mine(b5, b2)))
            def _():
                sent(bbuf.at[4 + b5 * 2 + b2], last_ss.at[b5 * 2 + b2])

    @pl.when(has_outer)
    def _():
        sent(halo.at[1 - c], halo_ss.at[0])

    sent(halo.at[c], halo_ss.at[1])


def fused_body(volume, directions, light_dir, tf_center, tf_width, tf_height, tf_emission):
    slab, rows, cols = volume.shape
    devices = lax.axis_size("depth") * lax.axis_size("wide")
    f32 = jnp.float32
    vmem = pl.BlockSpec(memory_space=pltpu.VMEM)
    hbm = pl.BlockSpec(memory_space=pltpu.HBM)
    parameters = (
        directions, light_dir, tf_center, tf_width, tf_height, jnp.transpose(tf_emission, (2, 0, 1))
    )
    word = jnp.int32
    dma = pltpu.SemaphoreType.DMA
    return pl.pallas_call(
        functools.partial(kernel, slab * devices),
        out_shape=jax.ShapeDtypeStruct((2, 4, rows * cols // devices), f32),
        in_specs=[hbm] * 7,
        out_specs=vmem,
        scratch_shapes=[pltpu.VMEM(volume.shape, volume.dtype)]
        + [pltpu.SMEM(p.shape, p.dtype) for p in parameters]
        + [
            dma((6 + slab,)),
            pltpu.VMEM((slab + 2, cols // 128 + 2, rows + 16, 128), f32),
            pltpu.VMEM((2, QUARTERS, rows, LANES), volume.dtype),
            pltpu.VMEM((2, rows // 8, 8, 128), f32),
            pltpu.VMEM((8, 128), f32),
            pltpu.VMEM((30, 8, 128), f32),
            pltpu.VMEM((EARLY, 2 * TILES, 10, 8, 128), f32),
            pltpu.VMEM((2, CHUNKS, 2, 4, TILES, 8, 128), f32),
            pltpu.VMEM((CHUNKS, 2, 4, TILES, 8, 128), f32),
            pltpu.VMEM((7, 2 * QUARTERS, 2, 2, TILES, 8, 128), word),
            pltpu.VMEM((8, QUARTERS, 2, TILES, 8, 128), word),
            dma((2,)),
            dma((2, QUARTERS)),
            dma,
            dma((CHUNKS,)),
            dma((3,)),
            dma((3, 2 * QUARTERS)),
            dma((4,)),
            dma((4, QUARTERS)),
        ],
        compiler_params=pltpu.CompilerParams(
            collective_id=0, has_side_effects=True, vmem_limit_bytes=67043328
        ),
    )(volume, *parameters)


def body(volume, *parameters):
    slab, rows, cols = volume.shape
    fused = (
        lax.axis_size("depth") == 2
        and lax.axis_size("wide") == 16
        and slab >= 3
        and rows == 128
        and cols == QUARTERS * LANES
    )
    return (fused_body if fused else plain_body)(volume, *parameters)


def solution(mesh):
    return jax.shard_map(
        body,
        mesh=mesh,
        in_specs=(P(("depth", "wide"), None, None), P(), P(), P(), P(), P(), P()),
        out_specs=P(None, None, ("depth", "wide")),
        check_vma=False,
    )
```

```python
import functools
import math

import jax
import jax.numpy as jnp
from jax import lax
from jax.experimental import pallas as pl
from jax.experimental.pallas import tpu as pltpu
from jax.sharding import PartitionSpec as P

AMBIENT = 0.3
DIFFUSE = 0.7


def padded_2(block, sides, width):
    for axis, dim in sides:
        count = lax.axis_size(axis)
        forward = [(i, i + 1) for i in range(count - 1)]
        backward = [(target, source) for source, target in forward]
        low = lax.ppermute(
            lax.slice_in_dim(block, block.shape[dim] - width, None, axis=dim), axis, forward
        )
        high = lax.ppermute(lax.slice_in_dim(block, 0, width, axis=dim), axis, backward)
        block = jnp.concatenate([low, block, high], axis=dim)
    return block


def partner(block, axis, distance):
    count = lax.axis_size(axis)
    route = []
    for low in range(count):
        high = low | 1 << distance
        if high != low and high < count:
            route += [(low, high), (high, low)]
    return lax.ppermute(block, axis, route)


def shifted_diff(values, along_axis):
    padding = [(0, 0)] * values.ndim
    padding[along_axis] = (1, 1)
    padded = jnp.pad(values, padding)
    length_now = values.shape[along_axis]
    upper_part = lax.slice_in_dim(padded, 2, length_now + 2, 1, along_axis)
    lower_part = lax.slice_in_dim(padded, 0, length_now, 1, along_axis)
    return 0.5 * (upper_part - lower_part)


def layer_rgba(
    layer_below,
    center_layer,
    layer_above,
    light_dir,
    tf_center,
    tf_width,
    tf_height,
    tf_emission,
    depth_step,
):
    grad_z = 0.5 * (layer_above - layer_below)
    grad_y = shifted_diff(center_layer, 0)
    grad_x = shifted_diff(center_layer, 1)
    lighting = jnp.abs(
        grad_z[None] * light_dir[:, 0, None, None]
        + grad_y[None] * light_dir[:, 1, None, None]
        + grad_x[None] * light_dir[:, 2, None, None]
    )
    magnitude = jnp.sqrt(grad_x * grad_x + grad_y * grad_y + grad_z * grad_z + 1.0)
    shading = AMBIENT + DIFFUSE * lighting / magnitude[None]
    scaled = (center_layer[None, None] - tf_center[:, :, None, None]) / tf_width[:, :, None, None]
    bumps = jnp.exp(-scaled * scaled)
    density = jnp.sum(tf_height[:, :, None, None] * bumps, axis=1)
    weights = tf_height[:, :, None] * tf_emission
    tinted = jnp.einsum("vkc,vkhw->vchw", weights, bumps, precision=lax.Precision.HIGHEST)
    colour = depth_step * shading[:, None] * tinted
    opacity = 1.0 - jnp.exp(-depth_step * density)
    sample_rgba = jnp.concatenate([colour, opacity[:, None]], axis=1)
    return sample_rgba.reshape(sample_rgba.shape[0], 4, -1)


def over_ordered(lower_part, upper_part, flags):
    front_first = lower_part + (1.0 - lower_part[:, 3:4]) * upper_part
    back_first = upper_part + (1.0 - upper_part[:, 3:4]) * lower_part
    return jnp.where(flags, back_first, front_first)


def split_pair(values, along_axis):
    array_shape = values.shape
    new_shape = (
        array_shape[:along_axis] + (array_shape[along_axis] // 2, 2) + array_shape[along_axis + 1 :]
    )
    paired = values.reshape(new_shape)
    first_half = lax.index_in_dim(paired, 0, along_axis + 1, keepdims=False)
    second_half = lax.index_in_dim(paired, 1, along_axis + 1, keepdims=False)
    return (first_half, second_half)


def plain_body(volume, directions, light_dir, tf_center, tf_width, tf_height, tf_emission):
    depth_count = lax.axis_size("depth")
    wide_count = lax.axis_size("wide")
    slab_cells = volume.shape[0]
    depth_step = 1.0 / (slab_cells * depth_count * wide_count)
    view_count = light_dir.shape[0]
    pixel_count = volume.shape[1] * volume.shape[2]
    flags = jnp.repeat(directions == 1, volume.shape[2], axis=1)[:, None, :]
    padded = padded_2(volume, ((("depth", "wide"), 0),), 1)

    def advance(layer_index, composite):
        layers = lax.dynamic_slice_in_dim(padded, layer_index, 3, 0).astype(jnp.float32)
        sample_rgba = layer_rgba(
            layers[0],
            layers[1],
            layers[2],
            light_dir,
            tf_center,
            tf_width,
            tf_height,
            tf_emission,
            depth_step,
        )
        return over_ordered(composite, sample_rgba, flags)

    initial = jnp.zeros((view_count, 4, pixel_count), jnp.float32)
    slab_image = lax.fori_loop(0, slab_cells, advance, initial)
    block_pixels = pixel_count // (depth_count * wide_count)
    blocked = slab_image.reshape(view_count, 4, depth_count, wide_count, block_pixels)
    blocked_flags = flags.reshape(view_count, 1, depth_count, wide_count, block_pixels)
    wide_index = lax.axis_index("wide")
    depth_index = lax.axis_index("depth")
    merged = blocked
    merged_flags = blocked_flags
    for bit_number in range(wide_count.bit_length() - 1):
        own_bit = wide_index >> bit_number & 1
        first_half, second_half = split_pair(merged, 3)
        flag_first, flag_second = split_pair(merged_flags, 3)
        kept = jnp.where(own_bit == 0, first_half, second_half)
        outgoing = jnp.where(own_bit == 0, second_half, first_half)
        merged_flags = jnp.where(own_bit == 0, flag_first, flag_second)
        incoming = partner(outgoing, "wide", bit_number)
        merged = jnp.where(
            own_bit == 0,
            over_ordered(kept, incoming, merged_flags),
            over_ordered(incoming, kept, merged_flags),
        )
    range_image = jnp.squeeze(merged, 3)
    range_flags = jnp.squeeze(merged_flags, 3)
    merged = range_image
    merged_flags = range_flags
    for bit_number in range(depth_count.bit_length() - 1):
        own_bit = depth_index >> bit_number & 1
        first_half, second_half = split_pair(merged, 2)
        flag_first, flag_second = split_pair(merged_flags, 2)
        kept = jnp.where(own_bit == 0, first_half, second_half)
        outgoing = jnp.where(own_bit == 0, second_half, first_half)
        merged_flags = jnp.where(own_bit == 0, flag_first, flag_second)
        incoming = partner(outgoing, "depth", bit_number)
        merged = jnp.where(
            own_bit == 0,
            over_ordered(kept, incoming, merged_flags),
            over_ordered(incoming, kept, merged_flags),
        )
    final_block = jnp.squeeze(merged, 2)
    return final_block


MESH = pl.DeviceIdType.MESH
LOG2E = math.log2(math.e)
LANES = 256
TILES = LANES // 128
QUARTERS = 4
CHUNKS = 32
EARLY = 12
EARLY_SIDE, WHOLE_SIDE = 4, 4
GREET = 3
LAG_CORE, LAG_QUAD, LAG_LAST = 4, 5, 16
LAST_IN_LOOP = 1
CODE_SCALE = 2048.0
CODE_SHIFT = 26.0


def encode(first, second):
    def code(value):
        at = jnp.log2(value) * CODE_SCALE + (CODE_SHIFT * CODE_SCALE + 0.5)
        return jnp.clip(at, 0.0, 65535.0).astype(jnp.int32)

    return code(first) | (code(second) << 16)


def decode(word):
    low = (word & 65535).astype(jnp.float32)
    high = ((word >> 16) & 65535).astype(jnp.float32)
    return [part * (1.0 / CODE_SCALE) - CODE_SHIFT for part in (low, high)]


def composite(words, flag):
    logs = [decode(a) + decode(b) for a, b in words]
    thick = [jnp.exp2(part[3]) for part in logs]
    before = [jnp.zeros_like(thick[0])]
    for t in thick:
        before.append(before[-1] + t)
    total = before[-1]
    colours = None
    for s, part in enumerate(logs):
        hidden = jnp.where(flag, total - before[s + 1], before[s])
        terms = [jnp.exp2(part[ch] - hidden) for ch in range(3)]
        colours = terms if colours is None else [a + b for a, b in zip(colours, terms)]
    return colours, total


def kernel(
    layer_total,
    vol, dirs_in, light_in, center_in, width_in, height_in, tint_in,
    out,
    slabs, dirs, light, center, width, height, tint, in_sems,
    xf, halo, flagv, flago, cst, early, rbuf, cbuf, abuf, bbuf,
    halo_ss, halo_rs, core_ss, core_rs, quad_ss, quad_rs, last_ss, last_rs,
):
    slab, rows, cols = vol.shape
    step = 1.0 / layer_total
    x = lax.axis_index("depth")
    w = lax.axis_index("wide")
    c = lax.rem(w, 2)
    y = lax.rem(lax.div(w, 2), 2)
    z0 = lax.rem(lax.div(w, 4), 2)
    z1 = lax.div(w, 8)
    me = x * 16 + w
    quad = z0 * 2 + y
    half = x * 2 + z1
    core_peer = (x, w + 1 - 2 * c)

    def quad_dev(rel):
        ry = lax.rem(rel, 2)
        rz = lax.div(rel, 2)
        return (x, w + ry * (2 - 4 * y) + rz * (4 - 8 * z0))

    def last_dev(b5, b2):
        return (c, b5 * 8 + z0 * 4 + y * 2 + b2)

    def last_mine(b5, b2):
        return jnp.logical_and(x == c, jnp.logical_and(b5 == z1, b2 == c))

    outer = lax.rem(me + 31 + 2 * c, 32)
    outer_dev = (lax.div(outer, 16), lax.rem(outer, 16))
    has_outer = jnp.logical_or(jnp.logical_and(c == 0, me > 0), jnp.logical_and(c == 1, me < 31))

    given = (
        (dirs_in, dirs), (light_in, light), (center_in, center), (width_in, width),
        (height_in, height), (tint_in, tint),
    )
    small = [pltpu.make_async_copy(a, b, in_sems.at[n]) for n, (a, b) in enumerate(given)]

    def slab_copy(z):
        return pltpu.make_async_copy(vol.at[z], slabs.at[z], in_sems.at[6 + z])

    barrier = pltpu.get_barrier_semaphore()

    def greet(device):
        pl.semaphore_signal(barrier, inc=1, device_id=device, device_id_type=MESH)

    @pl.when(has_outer)
    def _():
        greet(outer_dev)

    for sx in range(2):
        for sz in range(2):
            @pl.when(jnp.logical_not(jnp.logical_and(x == c, jnp.logical_and(sx == x, sz == z1))))
            def _():
                greet((sx, sz * 8 + z0 * 4 + y * 2 + x))
    for rel in (3, 2, 1):
        greet(quad_dev(rel))
    greet(core_peer)
    for z in range(slab):
        slab_copy(z).start()
    for copy in small:
        copy.start()

    def halo_lanes(q):
        return pl.ds(pl.multiple_of(q * LANES, LANES), LANES)

    def outer_copy(q):
        return pltpu.make_async_remote_copy(
            src_ref=vol.at[c * (slab - 1), :, halo_lanes(q)], dst_ref=halo.at[1 - c, q],
            send_sem=halo_ss.at[0], recv_sem=halo_rs.at[0, q],
            device_id=outer_dev, device_id_type=MESH)

    def inner_copy(q):
        return pltpu.make_async_remote_copy(
            src_ref=vol.at[(1 - c) * (slab - 1), :, halo_lanes(q)], dst_ref=halo.at[c, q],
            send_sem=halo_ss.at[1], recv_sem=halo_rs.at[1, q],
            device_id=core_peer, device_id_type=MESH)

    blank_rows = jnp.zeros((8, 128), jnp.float32)

    def blank(z, carry):
        for b in range(rows // 8 + 2):
            xf[z, 0, b * 8:b * 8 + 8, :] = blank_rows
            xf[z, cols // 128 + 1, b * 8:b * 8 + 8, :] = blank_rows
        for t in range(cols // 128):
            xf[z, t + 1, 0:8, :] = blank_rows
            xf[z, t + 1, rows + 8:rows + 16, :] = blank_rows
        return carry

    lax.fori_loop(1, slab + 1, blank, 0)

    def pad(z, carry):
        slab_copy(z - 1).wait()

        def widen(b, inner):
            for t in range(cols // 128):
                for r in (0, 16):
                    xf[z, t + 1, pl.ds(pl.multiple_of(b * 32 + r + 8, 8), 16), :] = slabs[
                        z - 1, pl.ds(pl.multiple_of(b * 32 + r, 16), 16), t * 128:t * 128 + 128
                    ].astype(jnp.float32)
            return inner

        return lax.fori_loop(0, rows // 32, widen, carry)

    lax.fori_loop(1, slab + 1, pad, 0)

    for copy in small:
        copy.wait()
    for v in range(2):
        for k in range(4):
            full = lambda ref: jnp.full((8, 128), ref[v, k], jnp.float32)
            scale = math.sqrt(LOG2E) / full(width)
            cst[v * 15 + k] = scale
            cst[v * 15 + 4 + k] = scale * full(center)
            cst[v * 15 + 8 + k] = jnp.log(full(height) * (step * LOG2E)) * LOG2E
        for a in range(3):
            cst[v * 15 + 12 + a] = jnp.full((8, 128), DIFFUSE * light[v, a], jnp.float32)
    row_of = lax.broadcasted_iota(jnp.int32, (8, 128), 0)
    lane_of = lax.broadcasted_iota(jnp.int32, (8, 128), 1)

    def fill_flags(g, carry):
        for v in range(2):
            for i in range(8):
                flagv[v, g, i:i + 1, :] = jnp.full((1, 128), dirs[v, g * 8 + i].astype(jnp.float32))
        return carry

    lax.fori_loop(0, rows // 8, fill_flags, 0)
    value = jnp.zeros((8, 128), jnp.float32)
    for i in range(8):
        value = jnp.where(row_of == i, dirs[i // 4, me * 4 + i % 4].astype(jnp.float32), value)
    flago[...] = value

    def take_halo(side, present, copy, q):
        place = side * (slab + 1)

        @pl.when(present)
        def _():
            copy(q).wait_recv()
            for p in range(TILES):
                xf[place, q * TILES + p + 1, 8:rows + 8, :] = halo[
                    side, q, :, p * 128:p * 128 + 128].astype(jnp.float32)

        @pl.when(jnp.logical_not(present))
        def _():
            for p in range(TILES):
                xf[place, q * TILES + p + 1, 8:rows + 8, :] = jnp.zeros((rows, 128), jnp.float32)

    def where_is(k):
        m = jnp.where(k < 6, k, jnp.where(k < 30, lax.rem(k + 2, 8), k - 24))
        b = jnp.where(k < 6, 0, jnp.where(k < 30, lax.div(k + 2, 8), 4))
        own = m >= 6
        q = jnp.where(own, b - 1, b)
        b5 = jnp.where(own, m - 6, jnp.where(m >= 3, 1, 0))
        rel = jnp.where(own, 0, 3 - m + 3 * b5)
        odd = jnp.logical_or(rel == 1, rel == 3)
        to_y = jnp.where(odd, 1 - y, y)
        to_z = jnp.where(rel >= 2, 1 - z0, z0)
        return q, b5, rel, b5 * 4 + to_z * 2 + to_y

    def layer(z, t, r0, here, behind, ahead, flags, signs, run, sums):
        rows8 = pl.ds(r0, 8)
        left = xf[z, t, rows8, :]
        right = xf[z, t + 2, rows8, :]
        above = xf[z, t + 1, pl.ds(r0 - 1, 8), :]
        below = xf[z, t + 1, pl.ds(r0 + 1, 8), :]
        gz = ahead - behind
        gy = below - above
        gx = pltpu.roll(jnp.where(lane_of == 0, right, here), 127, 1) - pltpu.roll(
            jnp.where(lane_of == 127, left, here), 1, 1)
        inverse = lax.rsqrt(gx * gx + gy * gy + (gz * gz + 4.0))
        for v in range(2):
            dot = gz * cst[v * 15 + 12] + gy * cst[v * 15 + 13] + gx * cst[v * 15 + 14]
            shade = jnp.abs(dot) * inverse + AMBIENT
            bumps = []
            for b in range(4):
                u = here * cst[v * 15 + b] - cst[v * 15 + 4 + b]
                bumps.append(jnp.exp2(cst[v * 15 + 8 + b] - u * u))
            thick = (bumps[0] + bumps[1]) + (bumps[2] + bumps[3])
            if run[v] is None:
                later = signs[v] * thick
                weight = jnp.exp2(jnp.where(flags[v], later, 0.0)) * shade
            else:
                later = run[v] + signs[v] * thick
                weight = jnp.exp2(jnp.where(flags[v], later, run[v])) * shade
            run[v] = later
            if sums[v] is None:
                sums[v] = [weight * b for b in bumps]
            else:
                sums[v] = [s + weight * b for s, b in zip(sums[v], bumps)]

    def tile_place(q, g, t):
        h = jnp.where(t >= TILES, 1, 0)
        p = t - TILES * h
        row_tile = h * 8 + g
        return h, p, row_tile, q * TILES + p, pl.multiple_of(row_tile * 8 + 8, 8)

    def orient(row_tile):
        flags = [flagv[v, row_tile] > 0.5 for v in range(2)]
        return flags, [jnp.where(f, 1.0, -1.0) for f in flags]

    def inside(first, last, t, r0, flags, signs, run, sums):
        rows8 = pl.ds(r0, 8)
        behind = xf[first - 1, t + 1, rows8, :]
        here = xf[first, t + 1, rows8, :]
        for z in range(first, last + 1):
            ahead = xf[z + 1, t + 1, rows8, :]
            layer(z, t, r0, here, behind, ahead, flags, signs, run, sums)
            behind, here = here, ahead

    def begin(k):
        q, b5, rel, g = where_is(k)

        def tile(t):
            h, p, row_tile, lane_tile, r0 = tile_place(q, g, t)
            flags, signs = orient(row_tile)
            run, sums = [None, None], [None, None]
            inside(2, slab - 1, lane_tile, r0, flags, signs, run, sums)
            for v in range(2):
                for b in range(4):
                    early[k, t, v * 5 + b] = sums[v][b]
                early[k, t, v * 5 + 4] = run[v]

        def tiles(n, carry):
            for m in range(EARLY_SIDE):
                tile(n * EARLY_SIDE + m)
            return carry

        lax.fori_loop(0, 2 * TILES // EARLY_SIDE, tiles, 0)

    def finish(k, whole):
        q, b5, rel, g = where_is(k)

        def tile(t):
            h, p, row_tile, lane_tile, r0 = tile_place(q, g, t)
            flags, signs = orient(row_tile)
            run, sums = [None, None], [None, None]
            if whole:
                inside(1, slab, lane_tile, r0, flags, signs, run, sums)
            else:
                inside(1, 1, lane_tile, r0, flags, signs, run, sums)
                for v in range(2):
                    lift = jnp.exp2(run[v])
                    sums[v] = [s + lift * early[k, t, v * 5 + b] for b, s in enumerate(sums[v])]
                    run[v] = run[v] + early[k, t, v * 5 + 4]
                inside(slab, slab, lane_tile, r0, flags, signs, run, sums)
            for v in range(2):
                total = signs[v] * run[v]
                front = jnp.where(flags[v], jnp.exp2(-total), 1.0) * (1.0 / LOG2E)
                scaled = [s * front for s in sums[v]]
                for ch in range(3):
                    value = scaled[0] * tint[ch, v, 0]
                    for b in range(1, 4):
                        value = value + scaled[b] * tint[ch, v, b]
                    rbuf[h, k, v, ch, p] = value
                rbuf[h, k, v, 3, p] = total

        def tiles(n, carry):
            for m in range(side):
                tile(n * side + m)
            return carry

        side = WHOLE_SIDE if whole else 2
        lax.fori_loop(0, 2 * TILES // side, tiles, 0)

    def core_copy(k):
        return pltpu.make_async_remote_copy(
            src_ref=rbuf.at[1 - c, k], dst_ref=cbuf.at[k], send_sem=core_ss,
            recv_sem=core_rs.at[k], device_id=core_peer, device_id_type=MESH)

    def quad_copy(rel, n):
        return pltpu.make_async_remote_copy(
            src_ref=abuf.at[3 + rel, n], dst_ref=abuf.at[quad, n], send_sem=quad_ss.at[rel - 1],
            recv_sem=quad_rs.at[rel - 1, n], device_id=quad_dev(rel), device_id_type=MESH)

    def last_copy(b5, b2, q):
        return pltpu.make_async_remote_copy(
            src_ref=bbuf.at[4 + b5 * 2 + b2, q], dst_ref=bbuf.at[half, q],
            send_sem=last_ss.at[b5 * 2 + b2], recv_sem=last_rs.at[half, q],
            device_id=last_dev(b5, b2), device_id_type=MESH)

    side_of_core = c.astype(jnp.float32)

    def merge_core(k):
        q, b5, rel, g = where_is(k)
        n = b5 * QUARTERS + q
        slot = jnp.where(rel == 0, quad, 3 + rel)
        core_copy(k).wait_recv()
        for v in range(2):
            flag = jnp.abs(flagv[v, c * 8 + g] - side_of_core) > 0.5
            for p in range(TILES):
                mine = [rbuf[c, k, v, ch, p] for ch in range(4)]
                other = [cbuf[k, v, ch, p] for ch in range(4)]
                clear = jnp.exp2(-jnp.where(flag, other[3], mine[3]))
                for_mine = jnp.where(flag, clear, 1.0)
                for_other = jnp.where(flag, 1.0, clear)
                colour = [for_mine * mine[ch] + for_other * other[ch] for ch in range(3)]
                abuf[slot, n, v, 0, p] = encode(colour[0], colour[1])
                abuf[slot, n, v, 1, p] = encode(colour[2], mine[3] + other[3])

        @pl.when(rel > 0)
        def _():
            quad_copy(rel, n).start()

    def merge_quad(b5, q):
        n = b5 * QUARTERS + q
        for rel in (3, 2, 1):
            quad_copy(rel, n).wait_recv()
        g = b5 * 4 + quad
        slots = [jnp.where(last_mine(b5, b2), half, 4 + b5 * 2 + b2) for b2 in range(2)]
        for v in range(2):
            flag = flagv[v, c * 8 + g] > 0.5
            for p in range(TILES):
                colour, thick = composite(
                    [(abuf[s, n, v, 0, p], abuf[s, n, v, 1, p]) for s in range(4)], flag)
                first = encode(colour[0], colour[1])
                second = encode(colour[2], thick)
                for b2 in range(2):
                    bbuf[slots[b2], q, 0, p, v * 4:v * 4 + 4] = first[b2 * 4:b2 * 4 + 4]
                    bbuf[slots[b2], q, 1, p, v * 4:v * 4 + 4] = second[b2 * 4:b2 * 4 + 4]
        for b2 in range(2):
            @pl.when(jnp.logical_not(last_mine(b5, b2)))
            def _():
                last_copy(b5, b2, q).start()

    def last_arrived(s, q):
        return pltpu.make_async_remote_copy(
            src_ref=bbuf.at[4, q], dst_ref=bbuf.at[s, q], send_sem=last_ss.at[0],
            recv_sem=last_rs.at[s, q], device_id=core_peer, device_id_type=MESH)

    def merge_last(q):
        for s in range(4):
            @pl.when(jnp.logical_not(jnp.logical_and(x == c, half == s)))
            def _():
                last_arrived(s, q).wait_recv()
        flag = flago[...] > 0.5
        for p in range(TILES):
            colour, thick = composite(
                [(bbuf[s, q, 0, p], bbuf[s, q, 1, p]) for s in range(4)], flag)
            parts = colour + [1.0 - jnp.exp2(-thick)]
            for r in range(8):
                spot = pl.ds(pl.multiple_of((r % 4) * cols + q * LANES + p * 128, 128), 128)
                for ch in range(4):
                    out[r // 4, ch:ch + 1, spot] = parts[ch][r:r + 1, :]

    def open_up():
        pl.semaphore_wait(barrier, 7 + jnp.where(x == c, 0, 1) + jnp.where(has_outer, 1, 0))

    def send_halo(q):
        @pl.when(has_outer)
        def _():
            outer_copy(q).start()

        inner_copy(q).start()

    def before(k, carry):
        @pl.when(k == GREET)
        def _():
            open_up()

        @pl.when(k == GREET)
        def _():
            send_halo(0)

        @pl.when(k == GREET + 3)
        def _():
            send_halo(1)

        begin(k)
        return carry

    lax.fori_loop(0, EARLY, before, 0)

    def advance(i, carry):
        @pl.when(i < CHUNKS)
        def _():
            @pl.when(jnp.logical_or(i == 0, i == 3))
            def _():
                send_halo(2 + jnp.where(i == 3, 1, 0))

            @pl.when(jnp.logical_or(i == 0, jnp.logical_and(i < 24, lax.rem(i + 2, 8) == 0)))
            def _():
                q = where_is(i)[0]

                @pl.when(c == 0)
                def _():
                    take_halo(0, has_outer, outer_copy, q)
                    take_halo(1, i >= 0, inner_copy, q)

                @pl.when(c == 1)
                def _():
                    take_halo(0, i >= 0, inner_copy, q)
                    take_halo(1, has_outer, outer_copy, q)

            @pl.when(i < EARLY)
            def _():
                finish(i, False)

            @pl.when(i >= EARLY)
            def _():
                finish(i, True)

            core_copy(i).start()

        @pl.when(jnp.logical_and(i >= LAG_CORE, i < CHUNKS + LAG_CORE))
        def _():
            merge_core(i - LAG_CORE)

        @pl.when(jnp.logical_and(i >= LAG_QUAD, i < CHUNKS + LAG_QUAD))
        def _():
            q, b5, rel, g = where_is(i - LAG_QUAD)

            @pl.when(rel == 0)
            def _():
                merge_quad(b5, q)

        @pl.when(jnp.logical_and(i >= LAG_LAST, i < CHUNKS))
        def _():
            q, b5, rel, g = where_is(i - LAG_LAST)

            @pl.when(jnp.logical_and(rel == 0, jnp.logical_and(b5 == 1, q < LAST_IN_LOOP)))
            def _():
                merge_last(q)

        return carry

    lax.fori_loop(0, CHUNKS + LAG_QUAD, advance, 0)

    def close(q, carry):
        merge_last(q)
        return carry

    lax.fori_loop(LAST_IN_LOOP, QUARTERS, close, 0)

    def sent(ref, semaphore):
        pltpu.make_async_remote_copy(
            src_ref=ref, dst_ref=ref, send_sem=semaphore, recv_sem=core_rs.at[0],
            device_id=core_peer, device_id_type=MESH).wait_send()

    sent(rbuf.at[1 - c], core_ss)
    for rel in (1, 2, 3):
        sent(abuf.at[3 + rel], quad_ss.at[rel - 1])
    for b5 in range(2):
        for b2 in range(2):
            @pl.when(jnp.logical_not(last_mine(b5, b2)))
            def _():
                sent(bbuf.at[4 + b5 * 2 + b2], last_ss.at[b5 * 2 + b2])

    @pl.when(has_outer)
    def _():
        sent(halo.at[1 - c], halo_ss.at[0])

    sent(halo.at[c], halo_ss.at[1])


def fused_body(volume, directions, light_dir, tf_center, tf_width, tf_height, tf_emission):
    slab, rows, cols = volume.shape
    devices = lax.axis_size("depth") * lax.axis_size("wide")
    f32 = jnp.float32
    vmem = pl.BlockSpec(memory_space=pltpu.VMEM)
    hbm = pl.BlockSpec(memory_space=pltpu.HBM)
    parameters = (
        directions, light_dir, tf_center, tf_width, tf_height, jnp.transpose(tf_emission, (2, 0, 1))
    )
    word = jnp.int32
    dma = pltpu.SemaphoreType.DMA
    return pl.pallas_call(
        functools.partial(kernel, slab * devices),
        out_shape=jax.ShapeDtypeStruct((2, 4, rows * cols // devices), f32),
        in_specs=[hbm] * 7,
        out_specs=vmem,
        scratch_shapes=[pltpu.VMEM(volume.shape, volume.dtype)]
        + [pltpu.SMEM(p.shape, p.dtype) for p in parameters]
        + [
            dma((6 + slab,)),
            pltpu.VMEM((slab + 2, cols // 128 + 2, rows + 16, 128), f32),
            pltpu.VMEM((2, QUARTERS, rows, LANES), volume.dtype),
            pltpu.VMEM((2, rows // 8, 8, 128), f32),
            pltpu.VMEM((8, 128), f32),
            pltpu.VMEM((30, 8, 128), f32),
            pltpu.VMEM((EARLY, 2 * TILES, 10, 8, 128), f32),
            pltpu.VMEM((2, CHUNKS, 2, 4, TILES, 8, 128), f32),
            pltpu.VMEM((CHUNKS, 2, 4, TILES, 8, 128), f32),
            pltpu.VMEM((7, 2 * QUARTERS, 2, 2, TILES, 8, 128), word),
            pltpu.VMEM((8, QUARTERS, 2, TILES, 8, 128), word),
            dma((2,)),
            dma((2, QUARTERS)),
            dma,
            dma((CHUNKS,)),
            dma((3,)),
            dma((3, 2 * QUARTERS)),
            dma((4,)),
            dma((4, QUARTERS)),
        ],
        compiler_params=pltpu.CompilerParams(
            collective_id=0, has_side_effects=True, vmem_limit_bytes=67043328
        ),
    )(volume, *parameters)


def body(volume, *parameters):
    slab, rows, cols = volume.shape
    fused = (
        lax.axis_size("depth") == 2
        and lax.axis_size("wide") == 16
        and slab >= 3
        and rows == 128
        and cols == QUARTERS * LANES
    )
    return (fused_body if fused else plain_body)(volume, *parameters)


def solution(mesh):
    return jax.shard_map(
        body,
        mesh=mesh,
        in_specs=(P(("depth", "wide"), None, None), P(), P(), P(), P(), P(), P()),
        out_specs=P(None, None, ("depth", "wide")),
        check_vma=False,
    )
```

```python
import functools
import math

import jax
import jax.numpy as jnp
from jax import lax
from jax.experimental import pallas as pl
from jax.experimental.pallas import tpu as pltpu
from jax.sharding import PartitionSpec as P

AMBIENT = 0.3
DIFFUSE = 0.7


def padded_2(block, sides, width):
    for axis, dim in sides:
        count = lax.axis_size(axis)
        forward = [(i, i + 1) for i in range(count - 1)]
        backward = [(target, source) for source, target in forward]
        low = lax.ppermute(
            lax.slice_in_dim(block, block.shape[dim] - width, None, axis=dim), axis, forward
        )
        high = lax.ppermute(lax.slice_in_dim(block, 0, width, axis=dim), axis, backward)
        block = jnp.concatenate([low, block, high], axis=dim)
    return block


def partner(block, axis, distance):
    count = lax.axis_size(axis)
    route = []
    for low in range(count):
        high = low | 1 << distance
        if high != low and high < count:
            route += [(low, high), (high, low)]
    return lax.ppermute(block, axis, route)


def shifted_diff(values, along_axis):
    padding = [(0, 0)] * values.ndim
    padding[along_axis] = (1, 1)
    padded = jnp.pad(values, padding)
    length_now = values.shape[along_axis]
    upper_part = lax.slice_in_dim(padded, 2, length_now + 2, 1, along_axis)
    lower_part = lax.slice_in_dim(padded, 0, length_now, 1, along_axis)
    return 0.5 * (upper_part - lower_part)


def layer_rgba(
    layer_below,
    center_layer,
    layer_above,
    light_dir,
    tf_center,
    tf_width,
    tf_height,
    tf_emission,
    depth_step,
):
    grad_z = 0.5 * (layer_above - layer_below)
    grad_y = shifted_diff(center_layer, 0)
    grad_x = shifted_diff(center_layer, 1)
    lighting = jnp.abs(
        grad_z[None] * light_dir[:, 0, None, None]
        + grad_y[None] * light_dir[:, 1, None, None]
        + grad_x[None] * light_dir[:, 2, None, None]
    )
    magnitude = jnp.sqrt(grad_x * grad_x + grad_y * grad_y + grad_z * grad_z + 1.0)
    shading = AMBIENT + DIFFUSE * lighting / magnitude[None]
    scaled = (center_layer[None, None] - tf_center[:, :, None, None]) / tf_width[:, :, None, None]
    bumps = jnp.exp(-scaled * scaled)
    density = jnp.sum(tf_height[:, :, None, None] * bumps, axis=1)
    weights = tf_height[:, :, None] * tf_emission
    tinted = jnp.einsum("vkc,vkhw->vchw", weights, bumps, precision=lax.Precision.HIGHEST)
    colour = depth_step * shading[:, None] * tinted
    opacity = 1.0 - jnp.exp(-depth_step * density)
    sample_rgba = jnp.concatenate([colour, opacity[:, None]], axis=1)
    return sample_rgba.reshape(sample_rgba.shape[0], 4, -1)


def over_ordered(lower_part, upper_part, flags):
    front_first = lower_part + (1.0 - lower_part[:, 3:4]) * upper_part
    back_first = upper_part + (1.0 - upper_part[:, 3:4]) * lower_part
    return jnp.where(flags, back_first, front_first)


def split_pair(values, along_axis):
    array_shape = values.shape
    new_shape = (
        array_shape[:along_axis] + (array_shape[along_axis] // 2, 2) + array_shape[along_axis + 1 :]
    )
    paired = values.reshape(new_shape)
    first_half = lax.index_in_dim(paired, 0, along_axis + 1, keepdims=False)
    second_half = lax.index_in_dim(paired, 1, along_axis + 1, keepdims=False)
    return (first_half, second_half)


def plain_body(volume, directions, light_dir, tf_center, tf_width, tf_height, tf_emission):
    depth_count = lax.axis_size("depth")
    wide_count = lax.axis_size("wide")
    slab_cells = volume.shape[0]
    depth_step = 1.0 / (slab_cells * depth_count * wide_count)
    view_count = light_dir.shape[0]
    pixel_count = volume.shape[1] * volume.shape[2]
    flags = jnp.repeat(directions == 1, volume.shape[2], axis=1)[:, None, :]
    padded = padded_2(volume, ((("depth", "wide"), 0),), 1)

    def advance(layer_index, composite):
        layers = lax.dynamic_slice_in_dim(padded, layer_index, 3, 0).astype(jnp.float32)
        sample_rgba = layer_rgba(
            layers[0],
            layers[1],
            layers[2],
            light_dir,
            tf_center,
            tf_width,
            tf_height,
            tf_emission,
            depth_step,
        )
        return over_ordered(composite, sample_rgba, flags)

    initial = jnp.zeros((view_count, 4, pixel_count), jnp.float32)
    slab_image = lax.fori_loop(0, slab_cells, advance, initial)
    block_pixels = pixel_count // (depth_count * wide_count)
    blocked = slab_image.reshape(view_count, 4, depth_count, wide_count, block_pixels)
    blocked_flags = flags.reshape(view_count, 1, depth_count, wide_count, block_pixels)
    wide_index = lax.axis_index("wide")
    depth_index = lax.axis_index("depth")
    merged = blocked
    merged_flags = blocked_flags
    for bit_number in range(wide_count.bit_length() - 1):
        own_bit = wide_index >> bit_number & 1
        first_half, second_half = split_pair(merged, 3)
        flag_first, flag_second = split_pair(merged_flags, 3)
        kept = jnp.where(own_bit == 0, first_half, second_half)
        outgoing = jnp.where(own_bit == 0, second_half, first_half)
        merged_flags = jnp.where(own_bit == 0, flag_first, flag_second)
        incoming = partner(outgoing, "wide", bit_number)
        merged = jnp.where(
            own_bit == 0,
            over_ordered(kept, incoming, merged_flags),
            over_ordered(incoming, kept, merged_flags),
        )
    range_image = jnp.squeeze(merged, 3)
    range_flags = jnp.squeeze(merged_flags, 3)
    merged = range_image
    merged_flags = range_flags
    for bit_number in range(depth_count.bit_length() - 1):
        own_bit = depth_index >> bit_number & 1
        first_half, second_half = split_pair(merged, 2)
        flag_first, flag_second = split_pair(merged_flags, 2)
        kept = jnp.where(own_bit == 0, first_half, second_half)
        outgoing = jnp.where(own_bit == 0, second_half, first_half)
        merged_flags = jnp.where(own_bit == 0, flag_first, flag_second)
        incoming = partner(outgoing, "depth", bit_number)
        merged = jnp.where(
            own_bit == 0,
            over_ordered(kept, incoming, merged_flags),
            over_ordered(incoming, kept, merged_flags),
        )
    final_block = jnp.squeeze(merged, 2)
    return final_block


MESH = pl.DeviceIdType.MESH
LOG2E = math.log2(math.e)
LANES = 256
TILES = LANES // 128
QUARTERS = 4
CHUNKS = 32
EARLY = 12
EARLY_SIDE, WHOLE_SIDE = 4, 4
GREET = 3
LAG_CORE, LAG_QUAD, LAG_LAST = 4, 5, 16
LAST_IN_LOOP = 1
LAG_FIRST = 8
CODE_SCALE = 2048.0
CODE_SHIFT = 26.0


def encode(first, second):
    def code(value):
        at = jnp.log2(value) * CODE_SCALE + (CODE_SHIFT * CODE_SCALE + 0.5)
        return jnp.clip(at, 0.0, 65535.0).astype(jnp.int32)

    return code(first) | (code(second) << 16)


def decode(word):
    low = (word & 65535).astype(jnp.float32)
    high = ((word >> 16) & 65535).astype(jnp.float32)
    return [part * (1.0 / CODE_SCALE) - CODE_SHIFT for part in (low, high)]


def composite(words, flag):
    logs = [decode(a) + decode(b) for a, b in words]
    thick = [jnp.exp2(part[3]) for part in logs]
    before = [jnp.zeros_like(thick[0])]
    for t in thick:
        before.append(before[-1] + t)
    total = before[-1]
    colours = None
    for s, part in enumerate(logs):
        hidden = jnp.where(flag, total - before[s + 1], before[s])
        terms = [jnp.exp2(part[ch] - hidden) for ch in range(3)]
        colours = terms if colours is None else [a + b for a, b in zip(colours, terms)]
    return colours, total


def kernel(
    layer_total,
    vol, dirs_in, light_in, center_in, width_in, height_in, tint_in,
    out,
    slabs, dirs, light, center, width, height, tint, in_sems,
    xf, halo, flagv, flago, cst, early, rbuf, cbuf, abuf, bbuf,
    halo_ss, halo_rs, core_ss, core_rs, quad_ss, quad_rs, last_ss, last_rs,
):
    slab, rows, cols = vol.shape
    step = 1.0 / layer_total
    x = lax.axis_index("depth")
    w = lax.axis_index("wide")
    c = lax.rem(w, 2)
    y = lax.rem(lax.div(w, 2), 2)
    z0 = lax.rem(lax.div(w, 4), 2)
    z1 = lax.div(w, 8)
    me = x * 16 + w
    quad = z0 * 2 + y
    half = x * 2 + z1
    core_peer = (x, w + 1 - 2 * c)

    def quad_dev(rel):
        ry = lax.rem(rel, 2)
        rz = lax.div(rel, 2)
        return (x, w + ry * (2 - 4 * y) + rz * (4 - 8 * z0))

    def last_dev(b5, b2):
        return (c, b5 * 8 + z0 * 4 + y * 2 + b2)

    def last_mine(b5, b2):
        return jnp.logical_and(x == c, jnp.logical_and(b5 == z1, b2 == c))

    outer = lax.rem(me + 31 + 2 * c, 32)
    outer_dev = (lax.div(outer, 16), lax.rem(outer, 16))
    has_outer = jnp.logical_or(jnp.logical_and(c == 0, me > 0), jnp.logical_and(c == 1, me < 31))

    given = (
        (dirs_in, dirs), (light_in, light), (center_in, center), (width_in, width),
        (height_in, height), (tint_in, tint),
    )
    small = [pltpu.make_async_copy(a, b, in_sems.at[n]) for n, (a, b) in enumerate(given)]

    def slab_copy(z):
        return pltpu.make_async_copy(vol.at[z], slabs.at[z], in_sems.at[6 + z])

    barrier = pltpu.get_barrier_semaphore()

    def greet(device):
        pl.semaphore_signal(barrier, inc=1, device_id=device, device_id_type=MESH)

    @pl.when(has_outer)
    def _():
        greet(outer_dev)

    for sx in range(2):
        for sz in range(2):
            @pl.when(jnp.logical_not(jnp.logical_and(x == c, jnp.logical_and(sx == x, sz == z1))))
            def _():
                greet((sx, sz * 8 + z0 * 4 + y * 2 + x))
    for rel in (3, 2, 1):
        greet(quad_dev(rel))
    greet(core_peer)
    for z in range(slab):
        slab_copy(z).start()
    for copy in small:
        copy.start()

    def halo_lanes(q):
        return pl.ds(pl.multiple_of(q * LANES, LANES), LANES)

    def outer_copy(q):
        return pltpu.make_async_remote_copy(
            src_ref=vol.at[c * (slab - 1), :, halo_lanes(q)], dst_ref=halo.at[1 - c, q],
            send_sem=halo_ss.at[0], recv_sem=halo_rs.at[0, q],
            device_id=outer_dev, device_id_type=MESH)

    def inner_copy(q):
        return pltpu.make_async_remote_copy(
            src_ref=vol.at[(1 - c) * (slab - 1), :, halo_lanes(q)], dst_ref=halo.at[c, q],
            send_sem=halo_ss.at[1], recv_sem=halo_rs.at[1, q],
            device_id=core_peer, device_id_type=MESH)

    blank_rows = jnp.zeros((8, 128), jnp.float32)

    def blank(z, carry):
        for b in range(rows // 8 + 2):
            xf[z, 0, b * 8:b * 8 + 8, :] = blank_rows
            xf[z, cols // 128 + 1, b * 8:b * 8 + 8, :] = blank_rows
        for t in range(cols // 128):
            xf[z, t + 1, 0:8, :] = blank_rows
            xf[z, t + 1, rows + 8:rows + 16, :] = blank_rows
        return carry

    lax.fori_loop(1, slab + 1, blank, 0)

    def pad(z, carry):
        slab_copy(z - 1).wait()

        def widen(b, inner):
            for t in range(cols // 128):
                for r in (0, 16):
                    xf[z, t + 1, pl.ds(pl.multiple_of(b * 32 + r + 8, 8), 16), :] = slabs[
                        z - 1, pl.ds(pl.multiple_of(b * 32 + r, 16), 16), t * 128:t * 128 + 128
                    ].astype(jnp.float32)
            return inner

        return lax.fori_loop(0, rows // 32, widen, carry)

    lax.fori_loop(1, slab + 1, pad, 0)

    for copy in small:
        copy.wait()
    for v in range(2):
        for k in range(4):
            full = lambda ref: jnp.full((8, 128), ref[v, k], jnp.float32)
            scale = math.sqrt(LOG2E) / full(width)
            cst[v * 15 + k] = scale
            cst[v * 15 + 4 + k] = scale * full(center)
            cst[v * 15 + 8 + k] = jnp.log(full(height) * (step * LOG2E)) * LOG2E
        for a in range(3):
            cst[v * 15 + 12 + a] = jnp.full((8, 128), DIFFUSE * light[v, a], jnp.float32)
    row_of = lax.broadcasted_iota(jnp.int32, (8, 128), 0)
    lane_of = lax.broadcasted_iota(jnp.int32, (8, 128), 1)

    def fill_flags(g, carry):
        for v in range(2):
            for i in range(8):
                flagv[v, g, i:i + 1, :] = jnp.full((1, 128), dirs[v, g * 8 + i].astype(jnp.float32))
        return carry

    lax.fori_loop(0, rows // 8, fill_flags, 0)
    value = jnp.zeros((8, 128), jnp.float32)
    for i in range(8):
        value = jnp.where(row_of == i, dirs[i // 4, me * 4 + i % 4].astype(jnp.float32), value)
    flago[...] = value

    def take_halo(side, present, copy, q):
        place = side * (slab + 1)

        @pl.when(present)
        def _():
            copy(q).wait_recv()
            for p in range(TILES):
                xf[place, q * TILES + p + 1, 8:rows + 8, :] = halo[
                    side, q, :, p * 128:p * 128 + 128].astype(jnp.float32)

        @pl.when(jnp.logical_not(present))
        def _():
            for p in range(TILES):
                xf[place, q * TILES + p + 1, 8:rows + 8, :] = jnp.zeros((rows, 128), jnp.float32)

    def where_is(k):
        m = jnp.where(k < 6, k, jnp.where(k < 30, lax.rem(k + 2, 8), k - 24))
        b = jnp.where(k < 6, 0, jnp.where(k < 30, lax.div(k + 2, 8), 4))
        own = m >= 6
        q = jnp.where(own, b - 1, b)
        b5 = jnp.where(own, m - 6, jnp.where(m >= 3, 1, 0))
        rel = jnp.where(own, 0, 3 - m + 3 * b5)
        odd = jnp.logical_or(rel == 1, rel == 3)
        to_y = jnp.where(odd, 1 - y, y)
        to_z = jnp.where(rel >= 2, 1 - z0, z0)
        return q, b5, rel, b5 * 4 + to_z * 2 + to_y

    def layer(z, t, r0, here, behind, ahead, flags, signs, run, sums):
        rows8 = pl.ds(r0, 8)
        left = xf[z, t, rows8, :]
        right = xf[z, t + 2, rows8, :]
        above = xf[z, t + 1, pl.ds(r0 - 1, 8), :]
        below = xf[z, t + 1, pl.ds(r0 + 1, 8), :]
        gz = ahead - behind
        gy = below - above
        gx = pltpu.roll(jnp.where(lane_of == 0, right, here), 127, 1) - pltpu.roll(
            jnp.where(lane_of == 127, left, here), 1, 1)
        inverse = lax.rsqrt(gx * gx + gy * gy + (gz * gz + 4.0))
        for v in range(2):
            dot = gz * cst[v * 15 + 12] + gy * cst[v * 15 + 13] + gx * cst[v * 15 + 14]
            shade = jnp.abs(dot) * inverse + AMBIENT
            bumps = []
            for b in range(4):
                u = here * cst[v * 15 + b] - cst[v * 15 + 4 + b]
                bumps.append(jnp.exp2(cst[v * 15 + 8 + b] - u * u))
            thick = (bumps[0] + bumps[1]) + (bumps[2] + bumps[3])
            if run[v] is None:
                later = signs[v] * thick
                weight = jnp.exp2(jnp.where(flags[v], later, 0.0)) * shade
            else:
                later = run[v] + signs[v] * thick
                weight = jnp.exp2(jnp.where(flags[v], later, run[v])) * shade
            run[v] = later
            if sums[v] is None:
                sums[v] = [weight * b for b in bumps]
            else:
                sums[v] = [s + weight * b for s, b in zip(sums[v], bumps)]

    def tile_place(q, g, t):
        h = jnp.where(t >= TILES, 1, 0)
        p = t - TILES * h
        row_tile = h * 8 + g
        return h, p, row_tile, q * TILES + p, pl.multiple_of(row_tile * 8 + 8, 8)

    def orient(row_tile):
        flags = [flagv[v, row_tile] > 0.5 for v in range(2)]
        return flags, [jnp.where(f, 1.0, -1.0) for f in flags]

    def inside(first, last, t, r0, flags, signs, run, sums):
        rows8 = pl.ds(r0, 8)
        behind = xf[first - 1, t + 1, rows8, :]
        here = xf[first, t + 1, rows8, :]
        for z in range(first, last + 1):
            ahead = xf[z + 1, t + 1, rows8, :]
            layer(z, t, r0, here, behind, ahead, flags, signs, run, sums)
            behind, here = here, ahead

    def begin(k):
        q, b5, rel, g = where_is(k)

        def tile(t):
            h, p, row_tile, lane_tile, r0 = tile_place(q, g, t)
            flags, signs = orient(row_tile)
            run, sums = [None, None], [None, None]
            inside(2, slab - 1, lane_tile, r0, flags, signs, run, sums)
            for v in range(2):
                for b in range(4):
                    early[k, t, v * 5 + b] = sums[v][b]
                early[k, t, v * 5 + 4] = run[v]

        def tiles(n, carry):
            for m in range(EARLY_SIDE):
                tile(n * EARLY_SIDE + m)
            return carry

        lax.fori_loop(0, 2 * TILES // EARLY_SIDE, tiles, 0)

    def finish(k, whole):
        q, b5, rel, g = where_is(k)

        def tile(t):
            h, p, row_tile, lane_tile, r0 = tile_place(q, g, t)
            flags, signs = orient(row_tile)
            run, sums = [None, None], [None, None]
            if whole:
                inside(1, slab, lane_tile, r0, flags, signs, run, sums)
            else:
                inside(1, 1, lane_tile, r0, flags, signs, run, sums)
                for v in range(2):
                    lift = jnp.exp2(run[v])
                    sums[v] = [s + lift * early[k, t, v * 5 + b] for b, s in enumerate(sums[v])]
                    run[v] = run[v] + early[k, t, v * 5 + 4]
                inside(slab, slab, lane_tile, r0, flags, signs, run, sums)
            for v in range(2):
                total = signs[v] * run[v]
                front = jnp.where(flags[v], jnp.exp2(-total), 1.0) * (1.0 / LOG2E)
                scaled = [s * front for s in sums[v]]
                for ch in range(3):
                    value = scaled[0] * tint[ch, v, 0]
                    for b in range(1, 4):
                        value = value + scaled[b] * tint[ch, v, b]
                    rbuf[h, k, v, ch, p] = value
                rbuf[h, k, v, 3, p] = total

        def tiles(n, carry):
            for m in range(side):
                tile(n * side + m)
            return carry

        side = WHOLE_SIDE if whole else 2
        lax.fori_loop(0, 2 * TILES // side, tiles, 0)

    def core_copy(k):
        return pltpu.make_async_remote_copy(
            src_ref=rbuf.at[1 - c, k], dst_ref=cbuf.at[k], send_sem=core_ss,
            recv_sem=core_rs.at[k], device_id=core_peer, device_id_type=MESH)

    def quad_copy(rel, n):
        return pltpu.make_async_remote_copy(
            src_ref=abuf.at[3 + rel, n], dst_ref=abuf.at[quad, n], send_sem=quad_ss.at[rel - 1],
            recv_sem=quad_rs.at[rel - 1, n], device_id=quad_dev(rel), device_id_type=MESH)

    def last_copy(b5, b2, q):
        return pltpu.make_async_remote_copy(
            src_ref=bbuf.at[4 + b5 * 2 + b2, q], dst_ref=bbuf.at[half, q],
            send_sem=last_ss.at[b5 * 2 + b2], recv_sem=last_rs.at[half, q],
            device_id=last_dev(b5, b2), device_id_type=MESH)

    side_of_core = c.astype(jnp.float32)

    def merge_core(k):
        q, b5, rel, g = where_is(k)
        n = b5 * QUARTERS + q
        slot = jnp.where(rel == 0, quad, 3 + rel)
        for v in range(2):
            flag = jnp.abs(flagv[v, c * 8 + g] - side_of_core) > 0.5
            for p in range(TILES):
                mine = [rbuf[c, k, v, ch, p] for ch in range(4)]
                other = [cbuf[k, v, ch, p] for ch in range(4)]
                clear = jnp.exp2(-jnp.where(flag, other[3], mine[3]))
                for_mine = jnp.where(flag, clear, 1.0)
                for_other = jnp.where(flag, 1.0, clear)
                colour = [for_mine * mine[ch] + for_other * other[ch] for ch in range(3)]
                abuf[slot, n, v, 0, p] = encode(colour[0], colour[1])
                abuf[slot, n, v, 1, p] = encode(colour[2], mine[3] + other[3])

    def pass_on(k):
        q, b5, rel, g = where_is(k)

        @pl.when(rel > 0)
        def _():
            quad_copy(rel, b5 * QUARTERS + q).start()

    def merge_quad(b5, q):
        n = b5 * QUARTERS + q
        for rel in (3, 2, 1):
            quad_copy(rel, n).wait_recv()
        g = b5 * 4 + quad
        slots = [jnp.where(last_mine(b5, b2), half, 4 + b5 * 2 + b2) for b2 in range(2)]
        for v in range(2):
            flag = flagv[v, c * 8 + g] > 0.5
            for p in range(TILES):
                colour, thick = composite(
                    [(abuf[s, n, v, 0, p], abuf[s, n, v, 1, p]) for s in range(4)], flag)
                first = encode(colour[0], colour[1])
                second = encode(colour[2], thick)
                for b2 in range(2):
                    bbuf[slots[b2], q, 0, p, v * 4:v * 4 + 4] = first[b2 * 4:b2 * 4 + 4]
                    bbuf[slots[b2], q, 1, p, v * 4:v * 4 + 4] = second[b2 * 4:b2 * 4 + 4]
        for b2 in range(2):
            @pl.when(jnp.logical_not(last_mine(b5, b2)))
            def _():
                last_copy(b5, b2, q).start()

    def last_arrived(s, q):
        return pltpu.make_async_remote_copy(
            src_ref=bbuf.at[4, q], dst_ref=bbuf.at[s, q], send_sem=last_ss.at[0],
            recv_sem=last_rs.at[s, q], device_id=core_peer, device_id_type=MESH)

    def merge_last(q):
        for s in range(4):
            @pl.when(jnp.logical_not(jnp.logical_and(x == c, half == s)))
            def _():
                last_arrived(s, q).wait_recv()
        flag = flago[...] > 0.5
        for p in range(TILES):
            colour, thick = composite(
                [(bbuf[s, q, 0, p], bbuf[s, q, 1, p]) for s in range(4)], flag)
            parts = colour + [1.0 - jnp.exp2(-thick)]
            for r in range(8):
                spot = pl.ds(pl.multiple_of((r % 4) * cols + q * LANES + p * 128, 128), 128)
                for ch in range(4):
                    out[r // 4, ch:ch + 1, spot] = parts[ch][r:r + 1, :]

    def open_up():
        pl.semaphore_wait(barrier, 7 + jnp.where(x == c, 0, 1) + jnp.where(has_outer, 1, 0))

    def send_halo(q):
        @pl.when(has_outer)
        def _():
            outer_copy(q).start()

        inner_copy(q).start()

    def before(k, carry):
        @pl.when(k == GREET)
        def _():
            open_up()

        @pl.when(k == GREET)
        def _():
            send_halo(0)

        @pl.when(k == GREET + 3)
        def _():
            send_halo(1)

        begin(k)
        return carry

    lax.fori_loop(0, EARLY, before, 0)

    def halos(i):
        q = where_is(i)[0]

        @pl.when(c == 0)
        def _():
            take_halo(0, has_outer, outer_copy, q)
            take_halo(1, i >= 0, inner_copy, q)

        @pl.when(c == 1)
        def _():
            take_halo(0, i >= 0, inner_copy, q)
            take_halo(1, has_outer, outer_copy, q)

    def merge_arrived(k):
        core_copy(k).wait_recv()
        merge_core(k)
        pass_on(k)

    def quad_step(k):
        q, b5, rel, g = where_is(k)

        @pl.when(rel == 0)
        def _():
            merge_quad(b5, q)

    def catch_up(i, carry):
        @pl.when(jnp.logical_or(i == 0, i == 3))
        def _():
            send_halo(2 + jnp.where(i == 3, 1, 0))

        @pl.when(jnp.logical_or(i == 0, i == 6))
        def _():
            halos(i)

        finish(i, False)
        core_copy(i).start()

        @pl.when(i >= LAG_CORE)
        def _():
            merge_arrived(i - LAG_CORE)

        return carry

    lax.fori_loop(0, EARLY, catch_up, 0)

    def advance(i, carry):
        @pl.when(jnp.logical_or(i == 14, i == 22))
        def _():
            halos(i)

        core_copy(i - LAG_CORE).wait_recv()
        merge_core(i - LAG_CORE)
        finish(i, True)
        core_copy(i).start()
        pass_on(i - LAG_CORE)
        quad_step(jnp.where(i < 14 + LAG_FIRST, i - LAG_FIRST, i - LAG_QUAD))

        @pl.when(i >= LAG_LAST)
        def _():
            q, b5, rel, g = where_is(i - LAG_LAST)

            @pl.when(jnp.logical_and(rel == 0, jnp.logical_and(b5 == 1, q < LAST_IN_LOOP)))
            def _():
                merge_last(q)

        return carry

    lax.fori_loop(EARLY, CHUNKS, advance, 0)

    def wind_down(i, carry):
        @pl.when(i < CHUNKS + LAG_CORE)
        def _():
            merge_arrived(i - LAG_CORE)

        quad_step(i - LAG_QUAD)
        return carry

    lax.fori_loop(CHUNKS, CHUNKS + LAG_QUAD, wind_down, 0)

    def close(q, carry):
        merge_last(q)
        return carry

    lax.fori_loop(LAST_IN_LOOP, QUARTERS, close, 0)

    def sent(ref, semaphore):
        pltpu.make_async_remote_copy(
            src_ref=ref, dst_ref=ref, send_sem=semaphore, recv_sem=core_rs.at[0],
            device_id=core_peer, device_id_type=MESH).wait_send()

    sent(rbuf.at[1 - c], core_ss)
    for rel in (1, 2, 3):
        sent(abuf.at[3 + rel], quad_ss.at[rel - 1])
    for b5 in range(2):
        for b2 in range(2):
            @pl.when(jnp.logical_not(last_mine(b5, b2)))
            def _():
                sent(bbuf.at[4 + b5 * 2 + b2], last_ss.at[b5 * 2 + b2])

    @pl.when(has_outer)
    def _():
        sent(halo.at[1 - c], halo_ss.at[0])

    sent(halo.at[c], halo_ss.at[1])


def fused_body(volume, directions, light_dir, tf_center, tf_width, tf_height, tf_emission):
    slab, rows, cols = volume.shape
    devices = lax.axis_size("depth") * lax.axis_size("wide")
    f32 = jnp.float32
    vmem = pl.BlockSpec(memory_space=pltpu.VMEM)
    hbm = pl.BlockSpec(memory_space=pltpu.HBM)
    parameters = (
        directions, light_dir, tf_center, tf_width, tf_height, jnp.transpose(tf_emission, (2, 0, 1))
    )
    word = jnp.int32
    dma = pltpu.SemaphoreType.DMA
    return pl.pallas_call(
        functools.partial(kernel, slab * devices),
        out_shape=jax.ShapeDtypeStruct((2, 4, rows * cols // devices), f32),
        in_specs=[hbm] * 7,
        out_specs=vmem,
        scratch_shapes=[pltpu.VMEM(volume.shape, volume.dtype)]
        + [pltpu.SMEM(p.shape, p.dtype) for p in parameters]
        + [
            dma((6 + slab,)),
            pltpu.VMEM((slab + 2, cols // 128 + 2, rows + 16, 128), f32),
            pltpu.VMEM((2, QUARTERS, rows, LANES), volume.dtype),
            pltpu.VMEM((2, rows // 8, 8, 128), f32),
            pltpu.VMEM((8, 128), f32),
            pltpu.VMEM((30, 8, 128), f32),
            pltpu.VMEM((EARLY, 2 * TILES, 10, 8, 128), f32),
            pltpu.VMEM((2, CHUNKS, 2, 4, TILES, 8, 128), f32),
            pltpu.VMEM((CHUNKS, 2, 4, TILES, 8, 128), f32),
            pltpu.VMEM((7, 2 * QUARTERS, 2, 2, TILES, 8, 128), word),
            pltpu.VMEM((8, QUARTERS, 2, TILES, 8, 128), word),
            dma((2,)),
            dma((2, QUARTERS)),
            dma,
            dma((CHUNKS,)),
            dma((3,)),
            dma((3, 2 * QUARTERS)),
            dma((4,)),
            dma((4, QUARTERS)),
        ],
        compiler_params=pltpu.CompilerParams(
            collective_id=0, has_side_effects=True, vmem_limit_bytes=67043328
        ),
    )(volume, *parameters)


def body(volume, *parameters):
    slab, rows, cols = volume.shape
    fused = (
        lax.axis_size("depth") == 2
        and lax.axis_size("wide") == 16
        and slab >= 3
        and rows == 128
        and cols == QUARTERS * LANES
    )
    return (fused_body if fused else plain_body)(volume, *parameters)


def solution(mesh):
    return jax.shard_map(
        body,
        mesh=mesh,
        in_specs=(P(("depth", "wide"), None, None), P(), P(), P(), P(), P(), P()),
        out_specs=P(None, None, ("depth", "wide")),
        check_vma=False,
    )
```

```python
import functools
import math

import jax
import jax.numpy as jnp
from jax import lax
from jax.experimental import pallas as pl
from jax.experimental.pallas import tpu as pltpu
from jax.sharding import PartitionSpec as P

AMBIENT = 0.3
DIFFUSE = 0.7


def padded_2(block, sides, width):
    for axis, dim in sides:
        count = lax.axis_size(axis)
        forward = [(i, i + 1) for i in range(count - 1)]
        backward = [(target, source) for source, target in forward]
        low = lax.ppermute(
            lax.slice_in_dim(block, block.shape[dim] - width, None, axis=dim), axis, forward
        )
        high = lax.ppermute(lax.slice_in_dim(block, 0, width, axis=dim), axis, backward)
        block = jnp.concatenate([low, block, high], axis=dim)
    return block


def partner(block, axis, distance):
    count = lax.axis_size(axis)
    route = []
    for low in range(count):
        high = low | 1 << distance
        if high != low and high < count:
            route += [(low, high), (high, low)]
    return lax.ppermute(block, axis, route)


def shifted_diff(values, along_axis):
    padding = [(0, 0)] * values.ndim
    padding[along_axis] = (1, 1)
    padded = jnp.pad(values, padding)
    length_now = values.shape[along_axis]
    upper_part = lax.slice_in_dim(padded, 2, length_now + 2, 1, along_axis)
    lower_part = lax.slice_in_dim(padded, 0, length_now, 1, along_axis)
    return 0.5 * (upper_part - lower_part)


def layer_rgba(
    layer_below,
    center_layer,
    layer_above,
    light_dir,
    tf_center,
    tf_width,
    tf_height,
    tf_emission,
    depth_step,
):
    grad_z = 0.5 * (layer_above - layer_below)
    grad_y = shifted_diff(center_layer, 0)
    grad_x = shifted_diff(center_layer, 1)
    lighting = jnp.abs(
        grad_z[None] * light_dir[:, 0, None, None]
        + grad_y[None] * light_dir[:, 1, None, None]
        + grad_x[None] * light_dir[:, 2, None, None]
    )
    magnitude = jnp.sqrt(grad_x * grad_x + grad_y * grad_y + grad_z * grad_z + 1.0)
    shading = AMBIENT + DIFFUSE * lighting / magnitude[None]
    scaled = (center_layer[None, None] - tf_center[:, :, None, None]) / tf_width[:, :, None, None]
    bumps = jnp.exp(-scaled * scaled)
    density = jnp.sum(tf_height[:, :, None, None] * bumps, axis=1)
    weights = tf_height[:, :, None] * tf_emission
    tinted = jnp.einsum("vkc,vkhw->vchw", weights, bumps, precision=lax.Precision.HIGHEST)
    colour = depth_step * shading[:, None] * tinted
    opacity = 1.0 - jnp.exp(-depth_step * density)
    sample_rgba = jnp.concatenate([colour, opacity[:, None]], axis=1)
    return sample_rgba.reshape(sample_rgba.shape[0], 4, -1)


def over_ordered(lower_part, upper_part, flags):
    front_first = lower_part + (1.0 - lower_part[:, 3:4]) * upper_part
    back_first = upper_part + (1.0 - upper_part[:, 3:4]) * lower_part
    return jnp.where(flags, back_first, front_first)


def split_pair(values, along_axis):
    array_shape = values.shape
    new_shape = (
        array_shape[:along_axis] + (array_shape[along_axis] // 2, 2) + array_shape[along_axis + 1 :]
    )
    paired = values.reshape(new_shape)
    first_half = lax.index_in_dim(paired, 0, along_axis + 1, keepdims=False)
    second_half = lax.index_in_dim(paired, 1, along_axis + 1, keepdims=False)
    return (first_half, second_half)


def plain_body(volume, directions, light_dir, tf_center, tf_width, tf_height, tf_emission):
    depth_count = lax.axis_size("depth")
    wide_count = lax.axis_size("wide")
    slab_cells = volume.shape[0]
    depth_step = 1.0 / (slab_cells * depth_count * wide_count)
    view_count = light_dir.shape[0]
    pixel_count = volume.shape[1] * volume.shape[2]
    flags = jnp.repeat(directions == 1, volume.shape[2], axis=1)[:, None, :]
    padded = padded_2(volume, ((("depth", "wide"), 0),), 1)

    def advance(layer_index, composite):
        layers = lax.dynamic_slice_in_dim(padded, layer_index, 3, 0).astype(jnp.float32)
        sample_rgba = layer_rgba(
            layers[0],
            layers[1],
            layers[2],
            light_dir,
            tf_center,
            tf_width,
            tf_height,
            tf_emission,
            depth_step,
        )
        return over_ordered(composite, sample_rgba, flags)

    initial = jnp.zeros((view_count, 4, pixel_count), jnp.float32)
    slab_image = lax.fori_loop(0, slab_cells, advance, initial)
    block_pixels = pixel_count // (depth_count * wide_count)
    blocked = slab_image.reshape(view_count, 4, depth_count, wide_count, block_pixels)
    blocked_flags = flags.reshape(view_count, 1, depth_count, wide_count, block_pixels)
    wide_index = lax.axis_index("wide")
    depth_index = lax.axis_index("depth")
    merged = blocked
    merged_flags = blocked_flags
    for bit_number in range(wide_count.bit_length() - 1):
        own_bit = wide_index >> bit_number & 1
        first_half, second_half = split_pair(merged, 3)
        flag_first, flag_second = split_pair(merged_flags, 3)
        kept = jnp.where(own_bit == 0, first_half, second_half)
        outgoing = jnp.where(own_bit == 0, second_half, first_half)
        merged_flags = jnp.where(own_bit == 0, flag_first, flag_second)
        incoming = partner(outgoing, "wide", bit_number)
        merged = jnp.where(
            own_bit == 0,
            over_ordered(kept, incoming, merged_flags),
            over_ordered(incoming, kept, merged_flags),
        )
    range_image = jnp.squeeze(merged, 3)
    range_flags = jnp.squeeze(merged_flags, 3)
    merged = range_image
    merged_flags = range_flags
    for bit_number in range(depth_count.bit_length() - 1):
        own_bit = depth_index >> bit_number & 1
        first_half, second_half = split_pair(merged, 2)
        flag_first, flag_second = split_pair(merged_flags, 2)
        kept = jnp.where(own_bit == 0, first_half, second_half)
        outgoing = jnp.where(own_bit == 0, second_half, first_half)
        merged_flags = jnp.where(own_bit == 0, flag_first, flag_second)
        incoming = partner(outgoing, "depth", bit_number)
        merged = jnp.where(
            own_bit == 0,
            over_ordered(kept, incoming, merged_flags),
            over_ordered(incoming, kept, merged_flags),
        )
    final_block = jnp.squeeze(merged, 2)
    return final_block


MESH = pl.DeviceIdType.MESH
LOG2E = math.log2(math.e)
LANES = 256
TILES = LANES // 128
QUARTERS = 4
CHUNKS = 32
EARLY = 12
EARLY_SIDE, WHOLE_SIDE = 4, 4
GREET = 3
LAG_CORE, LAG_QUAD, LAG_LAST = 4, 5, 16
LAST_IN_LOOP = 1
LAG_FIRST = 8
CODE_SCALE = 2048.0
CODE_SHIFT = 26.0


def encode(first, second):
    def code(value):
        at = jnp.log2(value) * CODE_SCALE + (CODE_SHIFT * CODE_SCALE + 0.5)
        return jnp.clip(at, 0.0, 65535.0).astype(jnp.int32)

    return code(first) | (code(second) << 16)


def decode(word):
    low = (word & 65535).astype(jnp.float32)
    high = ((word >> 16) & 65535).astype(jnp.float32)
    return [part * (1.0 / CODE_SCALE) - CODE_SHIFT for part in (low, high)]


def composite(words, flag):
    logs = [decode(a) + decode(b) for a, b in words]
    thick = [jnp.exp2(part[3]) for part in logs]
    before = [jnp.zeros_like(thick[0])]
    for t in thick:
        before.append(before[-1] + t)
    total = before[-1]
    colours = None
    for s, part in enumerate(logs):
        hidden = jnp.where(flag, total - before[s + 1], before[s])
        terms = [jnp.exp2(part[ch] - hidden) for ch in range(3)]
        colours = terms if colours is None else [a + b for a, b in zip(colours, terms)]
    return colours, total


def kernel(
    layer_total,
    vol, dirs_in, light_in, center_in, width_in, height_in, tint_in,
    out,
    slabs, dirs, light, center, width, height, tint, in_sems,
    xf, halo, flagv, flago, cst, early, rbuf, cbuf, abuf, bbuf,
    halo_ss, halo_rs, core_ss, core_rs, quad_ss, quad_rs, last_ss, last_rs,
):
    slab, rows, cols = vol.shape
    step = 1.0 / layer_total
    x = lax.axis_index("depth")
    w = lax.axis_index("wide")
    c = lax.rem(w, 2)
    y = lax.rem(lax.div(w, 2), 2)
    z0 = lax.rem(lax.div(w, 4), 2)
    z1 = lax.div(w, 8)
    me = x * 16 + w
    quad = z0 * 2 + y
    half = x * 2 + z1
    core_peer = (x, w + 1 - 2 * c)

    def quad_dev(rel):
        ry = lax.rem(rel, 2)
        rz = lax.div(rel, 2)
        return (x, w + ry * (2 - 4 * y) + rz * (4 - 8 * z0))

    def last_dev(b5, b2):
        return (c, b5 * 8 + z0 * 4 + y * 2 + b2)

    def last_mine(b5, b2):
        return jnp.logical_and(x == c, jnp.logical_and(b5 == z1, b2 == c))

    outer = lax.rem(me + 31 + 2 * c, 32)
    outer_dev = (lax.div(outer, 16), lax.rem(outer, 16))
    has_outer = jnp.logical_or(jnp.logical_and(c == 0, me > 0), jnp.logical_and(c == 1, me < 31))

    given = (
        (dirs_in, dirs), (light_in, light), (center_in, center), (width_in, width),
        (height_in, height), (tint_in, tint),
    )
    small = [pltpu.make_async_copy(a, b, in_sems.at[n]) for n, (a, b) in enumerate(given)]

    def slab_copy(z):
        return pltpu.make_async_copy(vol.at[z], slabs.at[z], in_sems.at[6 + z])

    barrier = pltpu.get_barrier_semaphore()

    def greet(device):
        pl.semaphore_signal(barrier, inc=1, device_id=device, device_id_type=MESH)

    @pl.when(has_outer)
    def _():
        greet(outer_dev)

    for sx in range(2):
        for sz in range(2):
            @pl.when(jnp.logical_not(jnp.logical_and(x == c, jnp.logical_and(sx == x, sz == z1))))
            def _():
                greet((sx, sz * 8 + z0 * 4 + y * 2 + x))
    for rel in (3, 2, 1):
        greet(quad_dev(rel))
    greet(core_peer)
    for copy in small:
        copy.start()
    for z in range(slab):
        slab_copy(z).start()

    def halo_lanes(q):
        return pl.ds(pl.multiple_of(q * LANES, LANES), LANES)

    def outer_copy(q):
        return pltpu.make_async_remote_copy(
            src_ref=vol.at[c * (slab - 1), :, halo_lanes(q)], dst_ref=halo.at[1 - c, q],
            send_sem=halo_ss.at[0], recv_sem=halo_rs.at[0, q],
            device_id=outer_dev, device_id_type=MESH)

    def inner_copy(q):
        return pltpu.make_async_remote_copy(
            src_ref=vol.at[(1 - c) * (slab - 1), :, halo_lanes(q)], dst_ref=halo.at[c, q],
            send_sem=halo_ss.at[1], recv_sem=halo_rs.at[1, q],
            device_id=core_peer, device_id_type=MESH)

    blank_rows = jnp.zeros((8, 128), jnp.float32)

    def blank(z, carry):
        for b in range(rows // 8 + 2):
            xf[z, 0, b * 8:b * 8 + 8, :] = blank_rows
            xf[z, cols // 128 + 1, b * 8:b * 8 + 8, :] = blank_rows
        for t in range(cols // 128):
            xf[z, t + 1, 0:8, :] = blank_rows
            xf[z, t + 1, rows + 8:rows + 16, :] = blank_rows
        return carry

    lax.fori_loop(1, slab + 1, blank, 0)

    def pad(z, carry):
        slab_copy(z - 1).wait()

        def widen(b, inner):
            for t in range(cols // 128):
                for r in (0, 16):
                    xf[z, t + 1, pl.ds(pl.multiple_of(b * 32 + r + 8, 8), 16), :] = slabs[
                        z - 1, pl.ds(pl.multiple_of(b * 32 + r, 16), 16), t * 128:t * 128 + 128
                    ].astype(jnp.float32)
            return inner

        return lax.fori_loop(0, rows // 32, widen, carry)


    for copy in small:
        copy.wait()
    for v in range(2):
        for k in range(4):
            full = lambda ref: jnp.full((8, 128), ref[v, k], jnp.float32)
            scale = math.sqrt(LOG2E) / full(width)
            cst[v * 15 + k] = scale
            cst[v * 15 + 4 + k] = scale * full(center)
            cst[v * 15 + 8 + k] = jnp.log(full(height) * (step * LOG2E)) * LOG2E
        for a in range(3):
            cst[v * 15 + 12 + a] = jnp.full((8, 128), DIFFUSE * light[v, a], jnp.float32)
    row_of = lax.broadcasted_iota(jnp.int32, (8, 128), 0)
    lane_of = lax.broadcasted_iota(jnp.int32, (8, 128), 1)

    def fill_flags(g, carry):
        for v in range(2):
            for i in range(8):
                flagv[v, g, i:i + 1, :] = jnp.full((1, 128), dirs[v, g * 8 + i].astype(jnp.float32))
        return carry

    lax.fori_loop(0, rows // 8, fill_flags, 0)
    value = jnp.zeros((8, 128), jnp.float32)
    for i in range(8):
        value = jnp.where(row_of == i, dirs[i // 4, me * 4 + i % 4].astype(jnp.float32), value)
    flago[...] = value
    lax.fori_loop(1, slab + 1, pad, 0)

    def take_halo(side, present, copy, q):
        place = side * (slab + 1)

        @pl.when(present)
        def _():
            copy(q).wait_recv()
            for p in range(TILES):
                xf[place, q * TILES + p + 1, 8:rows + 8, :] = halo[
                    side, q, :, p * 128:p * 128 + 128].astype(jnp.float32)

        @pl.when(jnp.logical_not(present))
        def _():
            for p in range(TILES):
                xf[place, q * TILES + p + 1, 8:rows + 8, :] = jnp.zeros((rows, 128), jnp.float32)

    def where_is(k):
        m = jnp.where(k < 6, k, jnp.where(k < 30, lax.rem(k + 2, 8), k - 24))
        b = jnp.where(k < 6, 0, jnp.where(k < 30, lax.div(k + 2, 8), 4))
        own = m >= 6
        q = jnp.where(own, b - 1, b)
        b5 = jnp.where(own, m - 6, jnp.where(m >= 3, 1, 0))
        rel = jnp.where(own, 0, 3 - m + 3 * b5)
        odd = jnp.logical_or(rel == 1, rel == 3)
        to_y = jnp.where(odd, 1 - y, y)
        to_z = jnp.where(rel >= 2, 1 - z0, z0)
        return q, b5, rel, b5 * 4 + to_z * 2 + to_y

    def layer(z, t, r0, here, behind, ahead, flags, signs, run, sums):
        rows8 = pl.ds(r0, 8)
        left = xf[z, t, rows8, :]
        right = xf[z, t + 2, rows8, :]
        above = xf[z, t + 1, pl.ds(r0 - 1, 8), :]
        below = xf[z, t + 1, pl.ds(r0 + 1, 8), :]
        gz = ahead - behind
        gy = below - above
        gx = pltpu.roll(jnp.where(lane_of == 0, right, here), 127, 1) - pltpu.roll(
            jnp.where(lane_of == 127, left, here), 1, 1)
        inverse = lax.rsqrt(gx * gx + gy * gy + (gz * gz + 4.0))
        for v in range(2):
            dot = gz * cst[v * 15 + 12] + gy * cst[v * 15 + 13] + gx * cst[v * 15 + 14]
            shade = jnp.abs(dot) * inverse + AMBIENT
            bumps = []
            for b in range(4):
                u = here * cst[v * 15 + b] - cst[v * 15 + 4 + b]
                bumps.append(jnp.exp2(cst[v * 15 + 8 + b] - u * u))
            thick = (bumps[0] + bumps[1]) + (bumps[2] + bumps[3])
            if run[v] is None:
                later = signs[v] * thick
                weight = jnp.exp2(jnp.where(flags[v], later, 0.0)) * shade
            else:
                later = run[v] + signs[v] * thick
                weight = jnp.exp2(jnp.where(flags[v], later, run[v])) * shade
            run[v] = later
            if sums[v] is None:
                sums[v] = [weight * b for b in bumps]
            else:
                sums[v] = [s + weight * b for s, b in zip(sums[v], bumps)]

    def tile_place(q, g, t):
        h = jnp.where(t >= TILES, 1, 0)
        p = t - TILES * h
        row_tile = h * 8 + g
        return h, p, row_tile, q * TILES + p, pl.multiple_of(row_tile * 8 + 8, 8)

    def orient(row_tile):
        flags = [flagv[v, row_tile] > 0.5 for v in range(2)]
        return flags, [jnp.where(f, 1.0, -1.0) for f in flags]

    def inside(first, last, t, r0, flags, signs, run, sums):
        rows8 = pl.ds(r0, 8)
        behind = xf[first - 1, t + 1, rows8, :]
        here = xf[first, t + 1, rows8, :]
        for z in range(first, last + 1):
            ahead = xf[z + 1, t + 1, rows8, :]
            layer(z, t, r0, here, behind, ahead, flags, signs, run, sums)
            behind, here = here, ahead

    def begin(k):
        q, b5, rel, g = where_is(k)

        def tile(t):
            h, p, row_tile, lane_tile, r0 = tile_place(q, g, t)
            flags, signs = orient(row_tile)
            run, sums = [None, None], [None, None]
            inside(2, slab - 1, lane_tile, r0, flags, signs, run, sums)
            for v in range(2):
                for b in range(4):
                    early[k, t, v * 5 + b] = sums[v][b]
                early[k, t, v * 5 + 4] = run[v]

        def tiles(n, carry):
            for m in range(EARLY_SIDE):
                tile(n * EARLY_SIDE + m)
            return carry

        lax.fori_loop(0, 2 * TILES // EARLY_SIDE, tiles, 0)

    def finish(k, whole):
        q, b5, rel, g = where_is(k)

        def tile(t):
            h, p, row_tile, lane_tile, r0 = tile_place(q, g, t)
            flags, signs = orient(row_tile)
            run, sums = [None, None], [None, None]
            if whole:
                inside(1, slab, lane_tile, r0, flags, signs, run, sums)
            else:
                inside(1, 1, lane_tile, r0, flags, signs, run, sums)
                for v in range(2):
                    lift = jnp.exp2(run[v])
                    sums[v] = [s + lift * early[k, t, v * 5 + b] for b, s in enumerate(sums[v])]
                    run[v] = run[v] + early[k, t, v * 5 + 4]
                inside(slab, slab, lane_tile, r0, flags, signs, run, sums)
            for v in range(2):
                total = signs[v] * run[v]
                front = jnp.where(flags[v], jnp.exp2(-total), 1.0) * (1.0 / LOG2E)
                scaled = [s * front for s in sums[v]]
                for ch in range(3):
                    value = scaled[0] * tint[ch, v, 0]
                    for b in range(1, 4):
                        value = value + scaled[b] * tint[ch, v, b]
                    rbuf[h, k, v, ch, p] = value
                rbuf[h, k, v, 3, p] = total

        def tiles(n, carry):
            for m in range(side):
                tile(n * side + m)
            return carry

        side = WHOLE_SIDE if whole else 2
        lax.fori_loop(0, 2 * TILES // side, tiles, 0)

    def core_copy(k):
        return pltpu.make_async_remote_copy(
            src_ref=rbuf.at[1 - c, k], dst_ref=cbuf.at[k], send_sem=core_ss,
            recv_sem=core_rs.at[k], device_id=core_peer, device_id_type=MESH)

    def quad_copy(rel, n):
        return pltpu.make_async_remote_copy(
            src_ref=abuf.at[3 + rel, n], dst_ref=abuf.at[quad, n], send_sem=quad_ss.at[rel - 1],
            recv_sem=quad_rs.at[rel - 1, n], device_id=quad_dev(rel), device_id_type=MESH)

    def last_copy(b5, b2, q):
        return pltpu.make_async_remote_copy(
            src_ref=bbuf.at[4 + b5 * 2 + b2, q], dst_ref=bbuf.at[half, q],
            send_sem=last_ss.at[b5 * 2 + b2], recv_sem=last_rs.at[half, q],
            device_id=last_dev(b5, b2), device_id_type=MESH)

    side_of_core = c.astype(jnp.float32)

    def merge_core(k):
        q, b5, rel, g = where_is(k)
        n = b5 * QUARTERS + q
        slot = jnp.where(rel == 0, quad, 3 + rel)
        for v in range(2):
            flag = jnp.abs(flagv[v, c * 8 + g] - side_of_core) > 0.5
            for p in range(TILES):
                mine = [rbuf[c, k, v, ch, p] for ch in range(4)]
                other = [cbuf[k, v, ch, p] for ch in range(4)]
                clear = jnp.exp2(-jnp.where(flag, other[3], mine[3]))
                for_mine = jnp.where(flag, clear, 1.0)
                for_other = jnp.where(flag, 1.0, clear)
                colour = [for_mine * mine[ch] + for_other * other[ch] for ch in range(3)]
                abuf[slot, n, v, 0, p] = encode(colour[0], colour[1])
                abuf[slot, n, v, 1, p] = encode(colour[2], mine[3] + other[3])

    def pass_on(k):
        q, b5, rel, g = where_is(k)

        @pl.when(rel > 0)
        def _():
            quad_copy(rel, b5 * QUARTERS + q).start()

    def merge_quad(b5, q):
        n = b5 * QUARTERS + q
        for rel in (3, 2, 1):
            quad_copy(rel, n).wait_recv()
        g = b5 * 4 + quad
        slots = [jnp.where(last_mine(b5, b2), half, 4 + b5 * 2 + b2) for b2 in range(2)]
        for v in range(2):
            flag = flagv[v, c * 8 + g] > 0.5
            for p in range(TILES):
                colour, thick = composite(
                    [(abuf[s, n, v, 0, p], abuf[s, n, v, 1, p]) for s in range(4)], flag)
                first = encode(colour[0], colour[1])
                second = encode(colour[2], thick)
                for b2 in range(2):
                    bbuf[slots[b2], q, 0, p, v * 4:v * 4 + 4] = first[b2 * 4:b2 * 4 + 4]
                    bbuf[slots[b2], q, 1, p, v * 4:v * 4 + 4] = second[b2 * 4:b2 * 4 + 4]
        for b2 in range(2):
            @pl.when(jnp.logical_not(last_mine(b5, b2)))
            def _():
                last_copy(b5, b2, q).start()

    def last_arrived(s, q):
        return pltpu.make_async_remote_copy(
            src_ref=bbuf.at[4, q], dst_ref=bbuf.at[s, q], send_sem=last_ss.at[0],
            recv_sem=last_rs.at[s, q], device_id=core_peer, device_id_type=MESH)

    def merge_last(q):
        for s in range(4):
            @pl.when(jnp.logical_not(jnp.logical_and(x == c, half == s)))
            def _():
                last_arrived(s, q).wait_recv()
        flag = flago[...] > 0.5
        for p in range(TILES):
            colour, thick = composite(
                [(bbuf[s, q, 0, p], bbuf[s, q, 1, p]) for s in range(4)], flag)
            parts = colour + [1.0 - jnp.exp2(-thick)]
            for r in range(8):
                spot = pl.ds(pl.multiple_of((r % 4) * cols + q * LANES + p * 128, 128), 128)
                for ch in range(4):
                    out[r // 4, ch:ch + 1, spot] = parts[ch][r:r + 1, :]

    def open_up():
        pl.semaphore_wait(barrier, 7 + jnp.where(x == c, 0, 1) + jnp.where(has_outer, 1, 0))

    def send_halo(q):
        @pl.when(has_outer)
        def _():
            outer_copy(q).start()

        inner_copy(q).start()

    def before(k, carry):
        @pl.when(k == GREET)
        def _():
            open_up()

        @pl.when(k == GREET)
        def _():
            send_halo(0)

        @pl.when(k == GREET + 3)
        def _():
            send_halo(1)

        begin(k)
        return carry

    lax.fori_loop(0, EARLY, before, 0)

    def halos(i):
        q = where_is(i)[0]

        @pl.when(c == 0)
        def _():
            take_halo(0, has_outer, outer_copy, q)
            take_halo(1, i >= 0, inner_copy, q)

        @pl.when(c == 1)
        def _():
            take_halo(0, i >= 0, inner_copy, q)
            take_halo(1, has_outer, outer_copy, q)

    def merge_arrived(k):
        core_copy(k).wait_recv()
        merge_core(k)
        pass_on(k)

    def quad_step(k):
        q, b5, rel, g = where_is(k)

        @pl.when(rel == 0)
        def _():
            merge_quad(b5, q)

    def catch_up(i, carry):
        @pl.when(jnp.logical_or(i == 0, i == 3))
        def _():
            send_halo(2 + jnp.where(i == 3, 1, 0))

        @pl.when(jnp.logical_or(i == 0, i == 6))
        def _():
            halos(i)

        finish(i, False)
        core_copy(i).start()

        @pl.when(i >= LAG_CORE)
        def _():
            merge_arrived(i - LAG_CORE)

        return carry

    lax.fori_loop(0, EARLY, catch_up, 0)

    def advance(i, carry):
        @pl.when(jnp.logical_or(i == 14, i == 22))
        def _():
            halos(i)

        core_copy(i - LAG_CORE).wait_recv()
        merge_core(i - LAG_CORE)
        finish(i, True)
        core_copy(i).start()
        pass_on(i - LAG_CORE)
        quad_step(jnp.where(i < 14 + LAG_FIRST, i - LAG_FIRST, i - LAG_QUAD))

        @pl.when(i >= LAG_LAST)
        def _():
            q, b5, rel, g = where_is(i - LAG_LAST)

            @pl.when(jnp.logical_and(rel == 0, jnp.logical_and(b5 == 1, q < LAST_IN_LOOP)))
            def _():
                merge_last(q)

        return carry

    lax.fori_loop(EARLY, CHUNKS, advance, 0)

    def wind_down(i, carry):
        @pl.when(i < CHUNKS + LAG_CORE)
        def _():
            merge_arrived(i - LAG_CORE)

        quad_step(i - LAG_QUAD)
        return carry

    lax.fori_loop(CHUNKS, CHUNKS + LAG_QUAD, wind_down, 0)

    def close(q, carry):
        merge_last(q)
        return carry

    lax.fori_loop(LAST_IN_LOOP, QUARTERS, close, 0)

    def sent(ref, semaphore):
        pltpu.make_async_remote_copy(
            src_ref=ref, dst_ref=ref, send_sem=semaphore, recv_sem=core_rs.at[0],
            device_id=core_peer, device_id_type=MESH).wait_send()

    sent(rbuf.at[1 - c], core_ss)
    for rel in (1, 2, 3):
        sent(abuf.at[3 + rel], quad_ss.at[rel - 1])
    for b5 in range(2):
        for b2 in range(2):
            @pl.when(jnp.logical_not(last_mine(b5, b2)))
            def _():
                sent(bbuf.at[4 + b5 * 2 + b2], last_ss.at[b5 * 2 + b2])

    @pl.when(has_outer)
    def _():
        sent(halo.at[1 - c], halo_ss.at[0])

    sent(halo.at[c], halo_ss.at[1])


def fused_body(volume, directions, light_dir, tf_center, tf_width, tf_height, tf_emission):
    slab, rows, cols = volume.shape
    devices = lax.axis_size("depth") * lax.axis_size("wide")
    f32 = jnp.float32
    vmem = pl.BlockSpec(memory_space=pltpu.VMEM)
    hbm = pl.BlockSpec(memory_space=pltpu.HBM)
    parameters = (
        directions, light_dir, tf_center, tf_width, tf_height, jnp.transpose(tf_emission, (2, 0, 1))
    )
    word = jnp.int32
    dma = pltpu.SemaphoreType.DMA
    return pl.pallas_call(
        functools.partial(kernel, slab * devices),
        out_shape=jax.ShapeDtypeStruct((2, 4, rows * cols // devices), f32),
        in_specs=[hbm] * 7,
        out_specs=vmem,
        scratch_shapes=[pltpu.VMEM(volume.shape, volume.dtype)]
        + [pltpu.SMEM(p.shape, p.dtype) for p in parameters]
        + [
            dma((6 + slab,)),
            pltpu.VMEM((slab + 2, cols // 128 + 2, rows + 16, 128), f32),
            pltpu.VMEM((2, QUARTERS, rows, LANES), volume.dtype),
            pltpu.VMEM((2, rows // 8, 8, 128), f32),
            pltpu.VMEM((8, 128), f32),
            pltpu.VMEM((30, 8, 128), f32),
            pltpu.VMEM((EARLY, 2 * TILES, 10, 8, 128), f32),
            pltpu.VMEM((2, CHUNKS, 2, 4, TILES, 8, 128), f32),
            pltpu.VMEM((CHUNKS, 2, 4, TILES, 8, 128), f32),
            pltpu.VMEM((7, 2 * QUARTERS, 2, 2, TILES, 8, 128), word),
            pltpu.VMEM((8, QUARTERS, 2, TILES, 8, 128), word),
            dma((2,)),
            dma((2, QUARTERS)),
            dma,
            dma((CHUNKS,)),
            dma((3,)),
            dma((3, 2 * QUARTERS)),
            dma((4,)),
            dma((4, QUARTERS)),
        ],
        compiler_params=pltpu.CompilerParams(
            collective_id=0, has_side_effects=True, vmem_limit_bytes=67043328
        ),
    )(volume, *parameters)


def body(volume, *parameters):
    slab, rows, cols = volume.shape
    fused = (
        lax.axis_size("depth") == 2
        and lax.axis_size("wide") == 16
        and slab >= 3
        and rows == 128
        and cols == QUARTERS * LANES
    )
    return (fused_body if fused else plain_body)(volume, *parameters)


def solution(mesh):
    return jax.shard_map(
        body,
        mesh=mesh,
        in_specs=(P(("depth", "wide"), None, None), P(), P(), P(), P(), P(), P()),
        out_specs=P(None, None, ("depth", "wide")),
        check_vma=False,
    )
```

```python
import functools
import math

import jax
import jax.numpy as jnp
from jax import lax
from jax.experimental import pallas as pl
from jax.experimental.pallas import tpu as pltpu
from jax.sharding import PartitionSpec as P

AMBIENT = 0.3
DIFFUSE = 0.7


def padded_2(block, sides, width):
    for axis, dim in sides:
        count = lax.axis_size(axis)
        forward = [(i, i + 1) for i in range(count - 1)]
        backward = [(target, source) for source, target in forward]
        low = lax.ppermute(
            lax.slice_in_dim(block, block.shape[dim] - width, None, axis=dim), axis, forward
        )
        high = lax.ppermute(lax.slice_in_dim(block, 0, width, axis=dim), axis, backward)
        block = jnp.concatenate([low, block, high], axis=dim)
    return block


def partner(block, axis, distance):
    count = lax.axis_size(axis)
    route = []
    for low in range(count):
        high = low | 1 << distance
        if high != low and high < count:
            route += [(low, high), (high, low)]
    return lax.ppermute(block, axis, route)


def shifted_diff(values, along_axis):
    padding = [(0, 0)] * values.ndim
    padding[along_axis] = (1, 1)
    padded = jnp.pad(values, padding)
    length_now = values.shape[along_axis]
    upper_part = lax.slice_in_dim(padded, 2, length_now + 2, 1, along_axis)
    lower_part = lax.slice_in_dim(padded, 0, length_now, 1, along_axis)
    return 0.5 * (upper_part - lower_part)


def layer_rgba(
    layer_below,
    center_layer,
    layer_above,
    light_dir,
    tf_center,
    tf_width,
    tf_height,
    tf_emission,
    depth_step,
):
    grad_z = 0.5 * (layer_above - layer_below)
    grad_y = shifted_diff(center_layer, 0)
    grad_x = shifted_diff(center_layer, 1)
    lighting = jnp.abs(
        grad_z[None] * light_dir[:, 0, None, None]
        + grad_y[None] * light_dir[:, 1, None, None]
        + grad_x[None] * light_dir[:, 2, None, None]
    )
    magnitude = jnp.sqrt(grad_x * grad_x + grad_y * grad_y + grad_z * grad_z + 1.0)
    shading = AMBIENT + DIFFUSE * lighting / magnitude[None]
    scaled = (center_layer[None, None] - tf_center[:, :, None, None]) / tf_width[:, :, None, None]
    bumps = jnp.exp(-scaled * scaled)
    density = jnp.sum(tf_height[:, :, None, None] * bumps, axis=1)
    weights = tf_height[:, :, None] * tf_emission
    tinted = jnp.einsum("vkc,vkhw->vchw", weights, bumps, precision=lax.Precision.HIGHEST)
    colour = depth_step * shading[:, None] * tinted
    opacity = 1.0 - jnp.exp(-depth_step * density)
    sample_rgba = jnp.concatenate([colour, opacity[:, None]], axis=1)
    return sample_rgba.reshape(sample_rgba.shape[0], 4, -1)


def over_ordered(lower_part, upper_part, flags):
    front_first = lower_part + (1.0 - lower_part[:, 3:4]) * upper_part
    back_first = upper_part + (1.0 - upper_part[:, 3:4]) * lower_part
    return jnp.where(flags, back_first, front_first)


def split_pair(values, along_axis):
    array_shape = values.shape
    new_shape = (
        array_shape[:along_axis] + (array_shape[along_axis] // 2, 2) + array_shape[along_axis + 1 :]
    )
    paired = values.reshape(new_shape)
    first_half = lax.index_in_dim(paired, 0, along_axis + 1, keepdims=False)
    second_half = lax.index_in_dim(paired, 1, along_axis + 1, keepdims=False)
    return (first_half, second_half)


def plain_body(volume, directions, light_dir, tf_center, tf_width, tf_height, tf_emission):
    depth_count = lax.axis_size("depth")
    wide_count = lax.axis_size("wide")
    slab_cells = volume.shape[0]
    depth_step = 1.0 / (slab_cells * depth_count * wide_count)
    view_count = light_dir.shape[0]
    pixel_count = volume.shape[1] * volume.shape[2]
    flags = jnp.repeat(directions == 1, volume.shape[2], axis=1)[:, None, :]
    padded = padded_2(volume, ((("depth", "wide"), 0),), 1)

    def advance(layer_index, composite):
        layers = lax.dynamic_slice_in_dim(padded, layer_index, 3, 0).astype(jnp.float32)
        sample_rgba = layer_rgba(
            layers[0],
            layers[1],
            layers[2],
            light_dir,
            tf_center,
            tf_width,
            tf_height,
            tf_emission,
            depth_step,
        )
        return over_ordered(composite, sample_rgba, flags)

    initial = jnp.zeros((view_count, 4, pixel_count), jnp.float32)
    slab_image = lax.fori_loop(0, slab_cells, advance, initial)
    block_pixels = pixel_count // (depth_count * wide_count)
    blocked = slab_image.reshape(view_count, 4, depth_count, wide_count, block_pixels)
    blocked_flags = flags.reshape(view_count, 1, depth_count, wide_count, block_pixels)
    wide_index = lax.axis_index("wide")
    depth_index = lax.axis_index("depth")
    merged = blocked
    merged_flags = blocked_flags
    for bit_number in range(wide_count.bit_length() - 1):
        own_bit = wide_index >> bit_number & 1
        first_half, second_half = split_pair(merged, 3)
        flag_first, flag_second = split_pair(merged_flags, 3)
        kept = jnp.where(own_bit == 0, first_half, second_half)
        outgoing = jnp.where(own_bit == 0, second_half, first_half)
        merged_flags = jnp.where(own_bit == 0, flag_first, flag_second)
        incoming = partner(outgoing, "wide", bit_number)
        merged = jnp.where(
            own_bit == 0,
            over_ordered(kept, incoming, merged_flags),
            over_ordered(incoming, kept, merged_flags),
        )
    range_image = jnp.squeeze(merged, 3)
    range_flags = jnp.squeeze(merged_flags, 3)
    merged = range_image
    merged_flags = range_flags
    for bit_number in range(depth_count.bit_length() - 1):
        own_bit = depth_index >> bit_number & 1
        first_half, second_half = split_pair(merged, 2)
        flag_first, flag_second = split_pair(merged_flags, 2)
        kept = jnp.where(own_bit == 0, first_half, second_half)
        outgoing = jnp.where(own_bit == 0, second_half, first_half)
        merged_flags = jnp.where(own_bit == 0, flag_first, flag_second)
        incoming = partner(outgoing, "depth", bit_number)
        merged = jnp.where(
            own_bit == 0,
            over_ordered(kept, incoming, merged_flags),
            over_ordered(incoming, kept, merged_flags),
        )
    final_block = jnp.squeeze(merged, 2)
    return final_block


MESH = pl.DeviceIdType.MESH
LOG2E = math.log2(math.e)
LANES = 256
TILES = LANES // 128
QUARTERS = 4
CHUNKS = 32
EARLY = 12
EARLY_SIDE, WHOLE_SIDE = 4, 4
GREET = 3
LAG_CORE, LAG_QUAD, LAG_LAST = 5, 6, 16
LAST_IN_LOOP = 1
LAG_FIRST = 8
CODE_SCALE = 2048.0
CODE_SHIFT = 26.0


def encode(first, second):
    def code(value):
        at = jnp.log2(value) * CODE_SCALE + (CODE_SHIFT * CODE_SCALE + 0.5)
        return jnp.clip(at, 0.0, 65535.0).astype(jnp.int32)

    return code(first) | (code(second) << 16)


def decode(word):
    low = (word & 65535).astype(jnp.float32)
    high = ((word >> 16) & 65535).astype(jnp.float32)
    return [part * (1.0 / CODE_SCALE) - CODE_SHIFT for part in (low, high)]


def composite(words, flag):
    logs = [decode(a) + decode(b) for a, b in words]
    thick = [jnp.exp2(part[3]) for part in logs]
    before = [jnp.zeros_like(thick[0])]
    for t in thick:
        before.append(before[-1] + t)
    total = before[-1]
    colours = None
    for s, part in enumerate(logs):
        hidden = jnp.where(flag, total - before[s + 1], before[s])
        terms = [jnp.exp2(part[ch] - hidden) for ch in range(3)]
        colours = terms if colours is None else [a + b for a, b in zip(colours, terms)]
    return colours, total


def kernel(
    layer_total,
    vol, dirs_in, light_in, center_in, width_in, height_in, tint_in,
    out,
    slabs, dirs, light, center, width, height, tint, in_sems,
    xf, halo, flagv, flago, cst, early, rbuf, cbuf, abuf, bbuf,
    halo_ss, halo_rs, core_ss, core_rs, quad_ss, quad_rs, last_ss, last_rs,
):
    slab, rows, cols = vol.shape
    step = 1.0 / layer_total
    x = lax.axis_index("depth")
    w = lax.axis_index("wide")
    c = lax.rem(w, 2)
    y = lax.rem(lax.div(w, 2), 2)
    z0 = lax.rem(lax.div(w, 4), 2)
    z1 = lax.div(w, 8)
    me = x * 16 + w
    quad = z0 * 2 + y
    half = x * 2 + z1
    core_peer = (x, w + 1 - 2 * c)

    def quad_dev(rel):
        ry = lax.rem(rel, 2)
        rz = lax.div(rel, 2)
        return (x, w + ry * (2 - 4 * y) + rz * (4 - 8 * z0))

    def last_dev(b5, b2):
        return (c, b5 * 8 + z0 * 4 + y * 2 + b2)

    def last_mine(b5, b2):
        return jnp.logical_and(x == c, jnp.logical_and(b5 == z1, b2 == c))

    outer = lax.rem(me + 31 + 2 * c, 32)
    outer_dev = (lax.div(outer, 16), lax.rem(outer, 16))
    has_outer = jnp.logical_or(jnp.logical_and(c == 0, me > 0), jnp.logical_and(c == 1, me < 31))

    given = (
        (dirs_in, dirs), (light_in, light), (center_in, center), (width_in, width),
        (height_in, height), (tint_in, tint),
    )
    small = [pltpu.make_async_copy(a, b, in_sems.at[n]) for n, (a, b) in enumerate(given)]

    def slab_copy(z):
        return pltpu.make_async_copy(vol.at[z], slabs.at[z], in_sems.at[6 + z])

    barrier = pltpu.get_barrier_semaphore()

    def greet(device):
        pl.semaphore_signal(barrier, inc=1, device_id=device, device_id_type=MESH)

    @pl.when(has_outer)
    def _():
        greet(outer_dev)

    for sx in range(2):
        for sz in range(2):
            @pl.when(jnp.logical_not(jnp.logical_and(x == c, jnp.logical_and(sx == x, sz == z1))))
            def _():
                greet((sx, sz * 8 + z0 * 4 + y * 2 + x))
    for rel in (3, 2, 1):
        greet(quad_dev(rel))
    greet(core_peer)
    for copy in small:
        copy.start()
    for z in range(slab):
        slab_copy(z).start()

    def halo_lanes(q):
        return pl.ds(pl.multiple_of(q * LANES, LANES), LANES)

    def outer_copy(q):
        return pltpu.make_async_remote_copy(
            src_ref=vol.at[c * (slab - 1), :, halo_lanes(q)], dst_ref=halo.at[1 - c, q],
            send_sem=halo_ss.at[0], recv_sem=halo_rs.at[0, q],
            device_id=outer_dev, device_id_type=MESH)

    def inner_copy(q):
        return pltpu.make_async_remote_copy(
            src_ref=vol.at[(1 - c) * (slab - 1), :, halo_lanes(q)], dst_ref=halo.at[c, q],
            send_sem=halo_ss.at[1], recv_sem=halo_rs.at[1, q],
            device_id=core_peer, device_id_type=MESH)

    blank_rows = jnp.zeros((8, 128), jnp.float32)

    def blank(z, carry):
        for b in range(rows // 8 + 2):
            xf[z, 0, b * 8:b * 8 + 8, :] = blank_rows
            xf[z, cols // 128 + 1, b * 8:b * 8 + 8, :] = blank_rows
        for t in range(cols // 128):
            xf[z, t + 1, 0:8, :] = blank_rows
            xf[z, t + 1, rows + 8:rows + 16, :] = blank_rows
        return carry

    lax.fori_loop(1, slab + 1, blank, 0)

    def pad(z, carry):
        slab_copy(z - 1).wait()

        def widen(b, inner):
            for t in range(cols // 128):
                for r in (0, 16):
                    xf[z, t + 1, pl.ds(pl.multiple_of(b * 32 + r + 8, 8), 16), :] = slabs[
                        z - 1, pl.ds(pl.multiple_of(b * 32 + r, 16), 16), t * 128:t * 128 + 128
                    ].astype(jnp.float32)
            return inner

        return lax.fori_loop(0, rows // 32, widen, carry)


    for copy in small:
        copy.wait()
    for v in range(2):
        for k in range(4):
            full = lambda ref: jnp.full((8, 128), ref[v, k], jnp.float32)
            scale = math.sqrt(LOG2E) / full(width)
            cst[v * 15 + k] = scale
            cst[v * 15 + 4 + k] = scale * full(center)
            cst[v * 15 + 8 + k] = jnp.log(full(height) * (step * LOG2E)) * LOG2E
        for a in range(3):
            cst[v * 15 + 12 + a] = jnp.full((8, 128), DIFFUSE * light[v, a], jnp.float32)
    row_of = lax.broadcasted_iota(jnp.int32, (8, 128), 0)
    lane_of = lax.broadcasted_iota(jnp.int32, (8, 128), 1)

    def fill_flags(g, carry):
        for v in range(2):
            for i in range(8):
                flagv[v, g, i:i + 1, :] = jnp.full((1, 128), dirs[v, g * 8 + i].astype(jnp.float32))
        return carry

    lax.fori_loop(0, rows // 8, fill_flags, 0)
    value = jnp.zeros((8, 128), jnp.float32)
    for i in range(8):
        value = jnp.where(row_of == i, dirs[i // 4, me * 4 + i % 4].astype(jnp.float32), value)
    flago[...] = value
    lax.fori_loop(1, slab + 1, pad, 0)

    def take_halo(side, present, copy, q):
        place = side * (slab + 1)

        @pl.when(present)
        def _():
            copy(q).wait_recv()
            for p in range(TILES):
                xf[place, q * TILES + p + 1, 8:rows + 8, :] = halo[
                    side, q, :, p * 128:p * 128 + 128].astype(jnp.float32)

        @pl.when(jnp.logical_not(present))
        def _():
            for p in range(TILES):
                xf[place, q * TILES + p + 1, 8:rows + 8, :] = jnp.zeros((rows, 128), jnp.float32)

    def where_is(k):
        m = jnp.where(k < 6, k, jnp.where(k < 30, lax.rem(k + 2, 8), k - 24))
        b = jnp.where(k < 6, 0, jnp.where(k < 30, lax.div(k + 2, 8), 4))
        own = m >= 6
        q = jnp.where(own, b - 1, b)
        b5 = jnp.where(own, m - 6, jnp.where(m >= 3, 1, 0))
        rel = jnp.where(own, 0, 3 - m + 3 * b5)
        odd = jnp.logical_or(rel == 1, rel == 3)
        to_y = jnp.where(odd, 1 - y, y)
        to_z = jnp.where(rel >= 2, 1 - z0, z0)
        return q, b5, rel, b5 * 4 + to_z * 2 + to_y

    def layer(z, t, r0, here, behind, ahead, flags, signs, run, sums):
        rows8 = pl.ds(r0, 8)
        left = xf[z, t, rows8, :]
        right = xf[z, t + 2, rows8, :]
        above = xf[z, t + 1, pl.ds(r0 - 1, 8), :]
        below = xf[z, t + 1, pl.ds(r0 + 1, 8), :]
        gz = ahead - behind
        gy = below - above
        gx = pltpu.roll(jnp.where(lane_of == 0, right, here), 127, 1) - pltpu.roll(
            jnp.where(lane_of == 127, left, here), 1, 1)
        inverse = lax.rsqrt(gx * gx + gy * gy + (gz * gz + 4.0))
        for v in range(2):
            dot = gz * cst[v * 15 + 12] + gy * cst[v * 15 + 13] + gx * cst[v * 15 + 14]
            shade = jnp.abs(dot) * inverse + AMBIENT
            bumps = []
            for b in range(4):
                u = here * cst[v * 15 + b] - cst[v * 15 + 4 + b]
                bumps.append(jnp.exp2(cst[v * 15 + 8 + b] - u * u))
            thick = (bumps[0] + bumps[1]) + (bumps[2] + bumps[3])
            if run[v] is None:
                later = signs[v] * thick
                weight = jnp.exp2(jnp.where(flags[v], later, 0.0)) * shade
            else:
                later = run[v] + signs[v] * thick
                weight = jnp.exp2(jnp.where(flags[v], later, run[v])) * shade
            run[v] = later
            if sums[v] is None:
                sums[v] = [weight * b for b in bumps]
            else:
                sums[v] = [s + weight * b for s, b in zip(sums[v], bumps)]

    def tile_place(q, g, t):
        h = jnp.where(t >= TILES, 1, 0)
        p = t - TILES * h
        row_tile = h * 8 + g
        return h, p, row_tile, q * TILES + p, pl.multiple_of(row_tile * 8 + 8, 8)

    def orient(row_tile):
        flags = [flagv[v, row_tile] > 0.5 for v in range(2)]
        return flags, [jnp.where(f, 1.0, -1.0) for f in flags]

    def inside(first, last, t, r0, flags, signs, run, sums):
        rows8 = pl.ds(r0, 8)
        behind = xf[first - 1, t + 1, rows8, :]
        here = xf[first, t + 1, rows8, :]
        for z in range(first, last + 1):
            ahead = xf[z + 1, t + 1, rows8, :]
            layer(z, t, r0, here, behind, ahead, flags, signs, run, sums)
            behind, here = here, ahead

    def begin(k):
        q, b5, rel, g = where_is(k)

        def tile(t):
            h, p, row_tile, lane_tile, r0 = tile_place(q, g, t)
            flags, signs = orient(row_tile)
            run, sums = [None, None], [None, None]
            inside(2, slab - 1, lane_tile, r0, flags, signs, run, sums)
            for v in range(2):
                for b in range(4):
                    early[k, t, v * 5 + b] = sums[v][b]
                early[k, t, v * 5 + 4] = run[v]

        def tiles(n, carry):
            for m in range(EARLY_SIDE):
                tile(n * EARLY_SIDE + m)
            return carry

        lax.fori_loop(0, 2 * TILES // EARLY_SIDE, tiles, 0)

    def finish(k, whole):
        q, b5, rel, g = where_is(k)

        def tile(t):
            h, p, row_tile, lane_tile, r0 = tile_place(q, g, t)
            flags, signs = orient(row_tile)
            run, sums = [None, None], [None, None]
            if whole:
                inside(1, slab, lane_tile, r0, flags, signs, run, sums)
            else:
                inside(1, 1, lane_tile, r0, flags, signs, run, sums)
                for v in range(2):
                    lift = jnp.exp2(run[v])
                    sums[v] = [s + lift * early[k, t, v * 5 + b] for b, s in enumerate(sums[v])]
                    run[v] = run[v] + early[k, t, v * 5 + 4]
                inside(slab, slab, lane_tile, r0, flags, signs, run, sums)
            for v in range(2):
                total = signs[v] * run[v]
                front = jnp.where(flags[v], jnp.exp2(-total), 1.0) * (1.0 / LOG2E)
                scaled = [s * front for s in sums[v]]
                for ch in range(3):
                    value = scaled[0] * tint[ch, v, 0]
                    for b in range(1, 4):
                        value = value + scaled[b] * tint[ch, v, b]
                    rbuf[h, k, v, ch, p] = value
                rbuf[h, k, v, 3, p] = total

        def tiles(n, carry):
            for m in range(side):
                tile(n * side + m)
            return carry

        side = WHOLE_SIDE if whole else 2
        lax.fori_loop(0, 2 * TILES // side, tiles, 0)

    def core_copy(k):
        return pltpu.make_async_remote_copy(
            src_ref=rbuf.at[1 - c, k], dst_ref=cbuf.at[k], send_sem=core_ss,
            recv_sem=core_rs.at[k], device_id=core_peer, device_id_type=MESH)

    def quad_copy(rel, n):
        return pltpu.make_async_remote_copy(
            src_ref=abuf.at[3 + rel, n], dst_ref=abuf.at[quad, n], send_sem=quad_ss.at[rel - 1],
            recv_sem=quad_rs.at[rel - 1, n], device_id=quad_dev(rel), device_id_type=MESH)

    def last_copy(b5, b2, q):
        return pltpu.make_async_remote_copy(
            src_ref=bbuf.at[4 + b5 * 2 + b2, q], dst_ref=bbuf.at[half, q],
            send_sem=last_ss.at[b5 * 2 + b2], recv_sem=last_rs.at[half, q],
            device_id=last_dev(b5, b2), device_id_type=MESH)

    side_of_core = c.astype(jnp.float32)

    def merge_core(k):
        q, b5, rel, g = where_is(k)
        n = b5 * QUARTERS + q
        slot = jnp.where(rel == 0, quad, 3 + rel)
        for v in range(2):
            flag = jnp.abs(flagv[v, c * 8 + g] - side_of_core) > 0.5
            for p in range(TILES):
                mine = [rbuf[c, k, v, ch, p] for ch in range(4)]
                other = [cbuf[k, v, ch, p] for ch in range(4)]
                clear = jnp.exp2(-jnp.where(flag, other[3], mine[3]))
                for_mine = jnp.where(flag, clear, 1.0)
                for_other = jnp.where(flag, 1.0, clear)
                colour = [for_mine * mine[ch] + for_other * other[ch] for ch in range(3)]
                abuf[slot, n, v, 0, p] = encode(colour[0], colour[1])
                abuf[slot, n, v, 1, p] = encode(colour[2], mine[3] + other[3])

    def pass_on(k):
        q, b5, rel, g = where_is(k)

        @pl.when(rel > 0)
        def _():
            quad_copy(rel, b5 * QUARTERS + q).start()

    def merge_quad(b5, q):
        n = b5 * QUARTERS + q
        for rel in (3, 2, 1):
            quad_copy(rel, n).wait_recv()
        g = b5 * 4 + quad
        slots = [jnp.where(last_mine(b5, b2), half, 4 + b5 * 2 + b2) for b2 in range(2)]
        for v in range(2):
            flag = flagv[v, c * 8 + g] > 0.5
            for p in range(TILES):
                colour, thick = composite(
                    [(abuf[s, n, v, 0, p], abuf[s, n, v, 1, p]) for s in range(4)], flag)
                first = encode(colour[0], colour[1])
                second = encode(colour[2], thick)
                for b2 in range(2):
                    bbuf[slots[b2], q, 0, p, v * 4:v * 4 + 4] = first[b2 * 4:b2 * 4 + 4]
                    bbuf[slots[b2], q, 1, p, v * 4:v * 4 + 4] = second[b2 * 4:b2 * 4 + 4]
        for b2 in range(2):
            @pl.when(jnp.logical_not(last_mine(b5, b2)))
            def _():
                last_copy(b5, b2, q).start()

    def last_arrived(s, q):
        return pltpu.make_async_remote_copy(
            src_ref=bbuf.at[4, q], dst_ref=bbuf.at[s, q], send_sem=last_ss.at[0],
            recv_sem=last_rs.at[s, q], device_id=core_peer, device_id_type=MESH)

    def merge_last(q):
        for s in range(4):
            @pl.when(jnp.logical_not(jnp.logical_and(x == c, half == s)))
            def _():
                last_arrived(s, q).wait_recv()
        flag = flago[...] > 0.5
        for p in range(TILES):
            colour, thick = composite(
                [(bbuf[s, q, 0, p], bbuf[s, q, 1, p]) for s in range(4)], flag)
            parts = colour + [1.0 - jnp.exp2(-thick)]
            for r in range(8):
                spot = pl.ds(pl.multiple_of((r % 4) * cols + q * LANES + p * 128, 128), 128)
                for ch in range(4):
                    out[r // 4, ch:ch + 1, spot] = parts[ch][r:r + 1, :]

    def open_up():
        pl.semaphore_wait(barrier, 7 + jnp.where(x == c, 0, 1) + jnp.where(has_outer, 1, 0))

    def send_halo(q):
        @pl.when(has_outer)
        def _():
            outer_copy(q).start()

        inner_copy(q).start()

    def before(k, carry):
        @pl.when(k == GREET)
        def _():
            open_up()

        @pl.when(k == GREET)
        def _():
            send_halo(0)

        @pl.when(k == GREET + 3)
        def _():
            send_halo(1)

        begin(k)
        return carry

    lax.fori_loop(0, EARLY, before, 0)

    def halos(i):
        q = where_is(i)[0]

        @pl.when(c == 0)
        def _():
            take_halo(0, has_outer, outer_copy, q)
            take_halo(1, i >= 0, inner_copy, q)

        @pl.when(c == 1)
        def _():
            take_halo(0, i >= 0, inner_copy, q)
            take_halo(1, has_outer, outer_copy, q)

    def merge_arrived(k):
        core_copy(k).wait_recv()
        merge_core(k)
        pass_on(k)

    def quad_step(k):
        q, b5, rel, g = where_is(k)

        @pl.when(rel == 0)
        def _():
            merge_quad(b5, q)

    def catch_up(i, carry):
        @pl.when(jnp.logical_or(i == 0, i == 3))
        def _():
            send_halo(2 + jnp.where(i == 3, 1, 0))

        @pl.when(jnp.logical_or(i == 0, i == 6))
        def _():
            halos(i)

        finish(i, False)
        core_copy(i).start()

        @pl.when(i >= LAG_CORE)
        def _():
            merge_arrived(i - LAG_CORE)

        return carry

    lax.fori_loop(0, EARLY, catch_up, 0)

    def advance(i, carry):
        @pl.when(jnp.logical_or(i == 14, i == 22))
        def _():
            halos(i)

        core_copy(i - LAG_CORE).wait_recv()
        merge_core(i - LAG_CORE)
        finish(i, True)
        core_copy(i).start()
        pass_on(i - LAG_CORE)
        quad_step(jnp.where(i < 14 + LAG_FIRST, i - LAG_FIRST, i - LAG_QUAD))

        @pl.when(i >= LAG_LAST)
        def _():
            q, b5, rel, g = where_is(i - LAG_LAST)

            @pl.when(jnp.logical_and(rel == 0, jnp.logical_and(b5 == 1, q < LAST_IN_LOOP)))
            def _():
                merge_last(q)

        return carry

    lax.fori_loop(EARLY, CHUNKS, advance, 0)

    def wind_down(i, carry):
        @pl.when(i < CHUNKS + LAG_CORE)
        def _():
            merge_arrived(i - LAG_CORE)

        quad_step(i - LAG_QUAD)
        return carry

    lax.fori_loop(CHUNKS, CHUNKS + LAG_QUAD, wind_down, 0)

    def close(q, carry):
        merge_last(q)
        return carry

    lax.fori_loop(LAST_IN_LOOP, QUARTERS, close, 0)

    def sent(ref, semaphore):
        pltpu.make_async_remote_copy(
            src_ref=ref, dst_ref=ref, send_sem=semaphore, recv_sem=core_rs.at[0],
            device_id=core_peer, device_id_type=MESH).wait_send()

    sent(rbuf.at[1 - c], core_ss)
    for rel in (1, 2, 3):
        sent(abuf.at[3 + rel], quad_ss.at[rel - 1])
    for b5 in range(2):
        for b2 in range(2):
            @pl.when(jnp.logical_not(last_mine(b5, b2)))
            def _():
                sent(bbuf.at[4 + b5 * 2 + b2], last_ss.at[b5 * 2 + b2])

    @pl.when(has_outer)
    def _():
        sent(halo.at[1 - c], halo_ss.at[0])

    sent(halo.at[c], halo_ss.at[1])


def fused_body(volume, directions, light_dir, tf_center, tf_width, tf_height, tf_emission):
    slab, rows, cols = volume.shape
    devices = lax.axis_size("depth") * lax.axis_size("wide")
    f32 = jnp.float32
    vmem = pl.BlockSpec(memory_space=pltpu.VMEM)
    hbm = pl.BlockSpec(memory_space=pltpu.HBM)
    parameters = (
        directions, light_dir, tf_center, tf_width, tf_height, jnp.transpose(tf_emission, (2, 0, 1))
    )
    word = jnp.int32
    dma = pltpu.SemaphoreType.DMA
    return pl.pallas_call(
        functools.partial(kernel, slab * devices),
        out_shape=jax.ShapeDtypeStruct((2, 4, rows * cols // devices), f32),
        in_specs=[hbm] * 7,
        out_specs=vmem,
        scratch_shapes=[pltpu.VMEM(volume.shape, volume.dtype)]
        + [pltpu.SMEM(p.shape, p.dtype) for p in parameters]
        + [
            dma((6 + slab,)),
            pltpu.VMEM((slab + 2, cols // 128 + 2, rows + 16, 128), f32),
            pltpu.VMEM((2, QUARTERS, rows, LANES), volume.dtype),
            pltpu.VMEM((2, rows // 8, 8, 128), f32),
            pltpu.VMEM((8, 128), f32),
            pltpu.VMEM((30, 8, 128), f32),
            pltpu.VMEM((EARLY, 2 * TILES, 10, 8, 128), f32),
            pltpu.VMEM((2, CHUNKS, 2, 4, TILES, 8, 128), f32),
            pltpu.VMEM((CHUNKS, 2, 4, TILES, 8, 128), f32),
            pltpu.VMEM((7, 2 * QUARTERS, 2, 2, TILES, 8, 128), word),
            pltpu.VMEM((8, QUARTERS, 2, TILES, 8, 128), word),
            dma((2,)),
            dma((2, QUARTERS)),
            dma,
            dma((CHUNKS,)),
            dma((3,)),
            dma((3, 2 * QUARTERS)),
            dma((4,)),
            dma((4, QUARTERS)),
        ],
        compiler_params=pltpu.CompilerParams(
            collective_id=0, has_side_effects=True, vmem_limit_bytes=67043328
        ),
    )(volume, *parameters)


def body(volume, *parameters):
    slab, rows, cols = volume.shape
    fused = (
        lax.axis_size("depth") == 2
        and lax.axis_size("wide") == 16
        and slab >= 3
        and rows == 128
        and cols == QUARTERS * LANES
    )
    return (fused_body if fused else plain_body)(volume, *parameters)


def solution(mesh):
    return jax.shard_map(
        body,
        mesh=mesh,
        in_specs=(P(("depth", "wide"), None, None), P(), P(), P(), P(), P(), P()),
        out_specs=P(None, None, ("depth", "wide")),
        check_vma=False,
    )
```
